32 devices in a mesh: dp: 4 (over z), tensor: 8 (over y, x, core).
Axes of the slice: x: 2, y: 2, z: 4, core: 2. Of those that a mesh axis runs over, the one named last changes fastest.
Arguments:
- gradients: bfloat16 [4, 64, 512, 512], P('dp', None, 'tensor'), may hold values from -240 to 240
- momentum: bfloat16 [4, 32, 512, 512], P('dp', None, 'tensor'), may hold values from -36 to 36
- owners: int32 [64], replicated, may hold values from 0 to 3, as said below
Outputs:
- updates: float32 [4, 32, 512, 512], P('dp', None, 'tensor')
The draws below stay inside these ranges and needn't reach their ends.
Inputs may be any that keep to these rules, and one draw needn't show every extreme that they name: `owners`: the blocks b with b // 16 == h give at most 8 blocks to any one owner, and exactly 8 to some owner, for every h; each owner holds at most 32 blocks, and some owner holds exactly 32.
All inputs are finite; a program needn't handle non-finite values.
Results may differ from the reference program's by a relative error of at most 0.018.
Values may be sent and summed in bfloat16 or wider, within the bound.
A program may use at most 64 MiB of HBM per device.

```python
import math
import jax
import jax.numpy as jnp
from jax import lax

BLOCK = 512
BPD = 16
ITERS = 3
NB = 64
PAIR = 8
MOST = 32
N_DP = 4


def draw_gradients(key, part):
    folded = jax.random.fold_in(key, 11)
    row_key, col_key, own_key = jax.random.split(folded, 3)
    row_scale = jnp.exp(jax.random.uniform(row_key, (NB, BLOCK, 1), jnp.float32, 0.0, math.log(10.0)))
    col_scale = jnp.exp(jax.random.uniform(col_key, (NB, 1, BLOCK), jnp.float32, 0.0, math.log(10.0)))
    replica_ids = jnp.arange(N_DP, dtype=jnp.int32)[:, None]
    holder_ids = (jnp.arange(NB, dtype=jnp.int32) // BPD)[None, :]
    boost = jnp.where(replica_ids == holder_ids, 6.0, 1.0).astype(jnp.float32)[:, :, None, None]
    blended = jax.random.truncated_normal(own_key, -4.0, 4.0, (N_DP, NB, BLOCK, BLOCK), jnp.float32) * boost
    return (0.1 * blended * row_scale[None] * col_scale[None]).astype(jnp.bfloat16)


def draw_owners(key, part):
    folded = jax.random.fold_in(key, 5)
    busiest = jax.random.randint(jax.random.fold_in(folded, 1), (), 0, N_DP).astype(jnp.int32)

    def one_group(group_key):
        pick_key, mix_key = jax.random.split(group_key)
        tickets = jax.random.permutation(pick_key, (N_DP - 1) * PAIR)[:BPD - PAIR].astype(jnp.int32)
        others = tickets // PAIR
        others = others + (others >= busiest).astype(jnp.int32)
        assigned = jnp.concatenate([jnp.full((PAIR,), busiest, jnp.int32), others.astype(jnp.int32)])
        return assigned[jax.random.permutation(mix_key, BPD)]
    group_keys = jax.random.split(jax.random.fold_in(folded, 2), N_DP)
    return jax.vmap(one_group)(group_keys).reshape(NB).astype(jnp.int32)


def shard_levels(key, extent, shards, smallest, top_value):
    factor_of, own = 1.0, jax.random.fold_in(key, 6)
    for dim, parts in shards:
        draws = jnp.exp(jax.random.uniform(jax.random.fold_in(own, dim), (parts,), jnp.float32, smallest / len(shards), top_value / len(shards)))
        factor_of = factor_of * jnp.repeat(draws, extent[dim] // parts).reshape([-1 if axis == dim else 1 for axis in range(len(extent))])
    return factor_of


def centred(stream_key, shape, deviation, most, cuts=(), kind=jnp.bfloat16):
    result = deviation * jax.random.normal(stream_key, shape, jnp.float32)
    if cuts:
        result = result * shard_levels(stream_key, shape, cuts, -0.22, 0.18)
    return jnp.clip(result, -most, most).astype(kind)


def setup_inputs(seed: int = 0) -> dict:
    arg_keys = jax.random.split(jax.random.key(seed), 4)
    gradients = draw_gradients(jax.random.fold_in(arg_keys[3], 71), 0)
    momentum = centred(arg_keys[1], (N_DP, MOST, BLOCK, BLOCK), 6.0, 36.0, ((0, 4), (2, 8)))
    owners = draw_owners(jax.random.fold_in(arg_keys[3], 71), 0)
    return {"gradients": gradients, "momentum": momentum, "owners": owners}


decay_rate = 0.95
newton_a = 3.4445
newton_b = -4.775
newton_c = 2.0315
norm_eps = 1e-07

def ranks_of(labels):
    length = labels.shape[0]
    places = jnp.arange(length, dtype=jnp.int32)
    earlier = (labels[None, :] == labels[:, None]) & (places[None, :] < places[:, None])
    return lax.optimization_barrier(jnp.sum(earlier.astype(jnp.int32), axis=1)).astype(jnp.int32)

def iterate_block(blended):
    widened = blended.astype(jnp.float32)
    length_sq = jnp.sum(widened * widened)
    current = widened / (jnp.sqrt(length_sq) + norm_eps)
    scale_up = math.sqrt(BLOCK)
    highest = lax.Precision.HIGHEST
    for iteration in range(ITERS):
        squared = jnp.dot(current, current.T, precision=highest, preferred_element_type=jnp.float32)
        polynomial = newton_b * squared + newton_c * jnp.dot(squared, squared, precision=highest, preferred_element_type=jnp.float32)
        current = newton_a * current + jnp.dot(polynomial, current, precision=highest, preferred_element_type=jnp.float32)
    return current * scale_up

def reference(gradients, momentum, owners):
    accumulated = gradients[0].astype(jnp.float32)
    for replica in range(1, N_DP):
        accumulated = accumulated + gradients[replica].astype(jnp.float32)
    summed = accumulated.astype(jnp.bfloat16)
    slot_rank = ranks_of(owners)

    def one_block(block_id):
        widened_g = summed[block_id].astype(jnp.float32)
        widened_m = momentum[owners[block_id], slot_rank[block_id]].astype(jnp.float32)
        blended = (widened_g + decay_rate * (decay_rate * widened_m + widened_g)).astype(jnp.bfloat16)
        return iterate_block(blended)
    finished = lax.map(one_block, jnp.arange(NB, dtype=jnp.int32))
    empty = jnp.zeros((N_DP, MOST, BLOCK, BLOCK), jnp.float32)
    return empty.at[owners, slot_rank].set(finished)
```

```python
import functools
import math

import jax
import jax.numpy as jnp
from jax import lax
from jax.experimental import pallas as pl
from jax.experimental.pallas import tpu as pltpu
from jax.sharding import PartitionSpec as P

ITERS = 3


decay_rate = 0.95
newton_a = 3.4445
newton_b = -4.775
newton_c = 2.0315
norm_eps = 1e-07


def ranks_of(labels):
    length = labels.shape[0]
    places = jnp.arange(length, dtype=jnp.int32)
    earlier = (labels[None, :] == labels[:, None]) & (places[None, :] < places[:, None])
    return jnp.sum(earlier.astype(jnp.int32), axis=1)


def rows_at(array, index):
    count = array.shape[0]
    chosen = (index[:, None] == jnp.arange(count, dtype=jnp.int32)[None, :]).astype(array.dtype)
    picked = jnp.dot(chosen, array.reshape(count, -1), preferred_element_type=jnp.float32)
    return picked.astype(array.dtype).reshape((index.shape[0],) + array.shape[1:])


def dot(spec, left, right):
    return jnp.einsum(
        spec,
        left.astype(jnp.bfloat16),
        right.astype(jnp.bfloat16),
        preferred_element_type=jnp.float32,
    )


def iterate(blocks):
    widened = blocks.astype(jnp.float32) * (1.0 + decay_rate)
    lengths = jnp.sqrt(jnp.sum(widened * widened, axis=(1, 2), keepdims=True)) + norm_eps
    current = widened / lengths
    scale_up = math.sqrt(blocks.shape[1])
    for iteration in range(ITERS):
        squared = dot("kij,klj->kil", current, current)
        polynomial = newton_b * squared + newton_c * dot("kij,kjl->kil", squared, squared)
        current = newton_a * current + dot("kij,kjl->kil", polynomial, current)
    return current * scale_up


def body(gradients, momentum, owners):
    dp_count = lax.axis_size("dp")
    tp_count = lax.axis_size("tensor")
    my_group = lax.axis_index("dp")
    pieces = gradients[0]
    blocks_all, rows, columns = pieces.shape
    per_group = blocks_all // dp_count
    capacity = momentum.shape[1]
    slot_rank = ranks_of(owners)
    places = jnp.arange(blocks_all, dtype=jnp.int32)

    mine = owners == my_group
    moment = rows_at(momentum[0], jnp.minimum(slot_rank, capacity - 1))
    moment = jnp.where(mine[:, None, None], moment, jnp.zeros_like(moment)).astype(jnp.float32)
    ratio = decay_rate * decay_rate / (1.0 + decay_rate)
    folded = (pieces.astype(jnp.float32) + ratio * moment).astype(jnp.bfloat16)
    held = lax.psum_scatter(folded, "dp", scatter_dimension=0, tiled=True)

    per_device = (per_group + tp_count - 1) // tp_count
    padded_count = per_device * tp_count
    padded = jnp.pad(held, ((0, padded_count - per_group), (0, 0), (0, 0)))
    whole = lax.all_to_all(padded, "tensor", split_axis=0, concat_axis=1, tiled=True)
    finished = iterate(whole).astype(jnp.bfloat16)
    result = lax.all_to_all(finished, "tensor", split_axis=1, concat_axis=0, tiled=True)

    groups = jnp.arange(dp_count, dtype=jnp.int32)
    pair_most = (2 * per_group + dp_count - 1) // dp_count
    held_owner = lax.dynamic_slice_in_dim(owners, my_group * per_group, per_group)
    held_rank = ranks_of(held_owner)
    held_places = jnp.arange(per_group, dtype=jnp.int32)
    pair_ids = jnp.arange(pair_most, dtype=jnp.int32)
    matched = (held_owner[:, None, None] == groups[None, :, None]) & (
        held_rank[:, None, None] == pair_ids[None, None, :]
    )
    source = jnp.sum(jnp.where(matched, held_places[:, None, None], 0), axis=0).reshape(-1)
    outgoing = rows_at(result, source)
    outgoing = outgoing.reshape(dp_count, pair_most, rows, columns)
    incoming = lax.all_to_all(outgoing, "dp", split_axis=0, concat_axis=0, tiled=True)
    incoming = incoming.reshape(dp_count * pair_most, rows, columns)
    group_rank = ranks_of(owners * dp_count + places // per_group)
    position = places // per_group * pair_most + group_rank
    slot_ids = jnp.arange(capacity, dtype=jnp.int32)
    my_slots = mine[:, None] & (slot_rank[:, None] == slot_ids[None, :])
    occupied = jnp.any(my_slots, axis=0)
    arriving = jnp.sum(jnp.where(my_slots, position[:, None], 0), axis=0)
    chosen = rows_at(incoming, arriving).astype(jnp.float32)
    update = jnp.where(occupied[:, None, None], chosen, jnp.zeros_like(chosen))
    return update[None]


MESH = pl.DeviceIdType.MESH


def kernel(
    sizes, weight, slot, g_ref, m_ref, out_ref,
    arrived, partial, whole, ready, gathered, current,
    chain_send, chain_recv, scatter_send, scatter_recv, return_send, ahead_send, gather_recv, out_sem,
):
    n, width, half, rows, lead = sizes
    columns = g_ref.shape[2]
    z, t = lax.axis_index("dp"), lax.axis_index("tensor")
    per_device = half // width
    gap = half
    is_end = (z == 0) | (z == n - 1)
    low = 2 * z < n - 1

    barrier = pltpu.get_barrier_semaphore()

    @pl.when(z > 0)
    def _():
        pl.semaphore_signal(barrier, inc=1, device_id=(z - 1, t), device_id_type=MESH)

    @pl.when(z < n - 1)
    def _():
        pl.semaphore_signal(barrier, inc=1, device_id=(z + 1, t), device_id_type=MESH)

    def greet(k, carry):
        peer = lax.rem(t + k, width)
        pl.semaphore_signal(barrier, inc=1, device_id=(z, peer), device_id_type=MESH)
        return carry

    lax.fori_loop(1, width, greet, 0)
    pl.semaphore_wait(barrier, jnp.where(is_end, width, width + 1))

    def chain_copy(d, c):
        return pltpu.make_async_remote_copy(
            src_ref=partial.at[d, c],
            dst_ref=arrived.at[d, c],
            send_sem=chain_send.at[d, c],
            recv_sem=chain_recv.at[d, c],
            device_id=(z + 2 * d - 1, t),
            device_id_type=MESH,
        )

    def own(d, c):
        block = d * half + c
        moment = m_ref[slot[block]].astype(jnp.float32)
        return g_ref[block].astype(jnp.float32) + weight[block] * moment

    def my_rows(place):
        return pl.ds(pl.multiple_of(place * rows, rows), rows)

    def start_chain(d, c):
        partial[d, c] = own(d, c).astype(jnp.bfloat16)
        chain_copy(d, c).start()

    def add_chain(d, c):
        chain_copy(d, c).wait_recv()
        total = own(d, c) + arrived[d, c].astype(jnp.float32)
        partial[d, c] = total.astype(jnp.bfloat16)

    def scatter_copy(d, c, peer, sem):
        return pltpu.make_async_remote_copy(
            src_ref=partial.at[d, c],
            dst_ref=whole.at[c // width, my_rows(t)],
            send_sem=scatter_send.at[c],
            recv_sem=sem,
            device_id=(z, peer),
            device_id_type=MESH,
        )

    def return_copy(d, j, peer):
        block = d * half + j * width + t
        return pltpu.make_async_remote_copy(
            src_ref=ready.at[j, my_rows(peer)],
            dst_ref=gathered.at[block],
            send_sem=return_send.at[j, peer],
            recv_sem=gather_recv.at[block],
            device_id=(z, peer),
            device_id_type=MESH,
        )

    def ahead_copy(d, c):
        block = d * half + c
        return pltpu.make_async_remote_copy(
            src_ref=gathered.at[block],
            dst_ref=gathered.at[block],
            send_sem=ahead_send.at[block],
            recv_sem=gather_recv.at[block],
            device_id=(z + 1 - 2 * d, t),
            device_id_type=MESH,
        )

    def pass_on(d, c):
        ahead_copy(d, c).wait_recv()

        @pl.when((z + 1 - 2 * d >= 0) & (z + 1 - 2 * d < n))
        def _():
            ahead_copy(d, c).start()

    def iterate_in(j):
        widened = whole[j].astype(jnp.float32) * (1.0 + decay_rate)
        length = jnp.sqrt(jnp.sum(widened * widened)) + norm_eps
        current[...] = widened / length

        def once(k, carry):
            now = current[...]
            low_now = now.astype(jnp.bfloat16)
            squared = lax.dot_general(
                low_now, low_now, (((1,), (1,)), ((), ())), preferred_element_type=jnp.float32
            )
            low_squared = squared.astype(jnp.bfloat16)
            polynomial = newton_b * squared + newton_c * jnp.dot(
                low_squared, low_squared, preferred_element_type=jnp.float32
            )
            current[...] = newton_a * now + jnp.dot(
                polynomial.astype(jnp.bfloat16), low_now, preferred_element_type=jnp.float32
            )
            return carry

        lax.fori_loop(0, ITERS, once, 0)
        ready[j] = (current[...] * math.sqrt(columns)).astype(jnp.bfloat16)

    @pl.when(is_end)
    def _():
        near = jnp.where(z == 0, 0, 1)
        far = 1 - near

        def begin(c, carry):
            start_chain(far, c)
            return carry

        lax.fori_loop(0, half, begin, 0)

        def pass_group(j):
            def one(k, inner):
                pass_on(near, j * width + k)
                return inner

            lax.fori_loop(0, width, one, 0)

        def reduce_group(j):
            def chunk(k, inner):
                c = j * width + k
                add_chain(near, c)

                @pl.when(k == t)
                def _():
                    pltpu.make_async_copy(
                        partial.at[near, c], whole.at[j, my_rows(t)], scatter_recv.at[j, t]
                    ).start()

                @pl.when(k != t)
                def _():
                    scatter_copy(near, c, k, scatter_recv.at[j, t]).start()

                return inner

            lax.fori_loop(0, width, chunk, 0)

        def iterate_group(j):
            def land(k, inner):
                pltpu.make_async_copy(
                    partial.at[near, 0], whole.at[j, my_rows(k)], scatter_recv.at[j, k]
                ).wait()
                return inner

            lax.fori_loop(0, width, land, 0)
            iterate_in(j)

            def give(k, inner):
                @pl.when(k == t)
                def _():
                    block = near * half + j * width + t
                    pltpu.make_async_copy(
                        ready.at[j, my_rows(t)], gathered.at[block], gather_recv.at[block]
                    ).start()

                @pl.when(k != t)
                def _():
                    return_copy(near, j, k).start()

                return inner

            lax.fori_loop(0, width, give, 0)

        def block_step(j, carry):
            @pl.when(j < per_device)
            def _():
                reduce_group(j)

            @pl.when(j > 1)
            def _():
                pass_group(j - 2)

            @pl.when(j > 0)
            def _():
                iterate_group(j - 1)

            return carry

        lax.fori_loop(0, per_device + 1, block_step, 0)
        pass_group(per_device - 1)

        def finish(c, carry):
            pass_on(far, c)
            return carry

        lax.fori_loop(0, half, finish, 0)

    @pl.when(jnp.logical_not(is_end))
    def _():
        early = jnp.where(low, 1, 0)

        def forward(d, c):
            add_chain(d, c)
            chain_copy(d, c).start()

        def step(i, carry):
            @pl.when(i < half)
            def _():
                forward(early, i)

            @pl.when((i >= lead) & (i < half + lead))
            def _():
                forward(1 - early, i - lead)

            @pl.when((i >= gap) & (i < half + gap))
            def _():
                pass_on(1 - early, i - gap)

            @pl.when(i >= gap + lead)
            def _():
                pass_on(early, i - gap - lead)

            return carry

        lax.fori_loop(0, half + gap + lead, step, 0)

    final = pltpu.make_async_copy(gathered, out_ref, out_sem)
    final.start()

    for d in range(2):
        sink = 0 if d == 0 else n - 1

        def settle(c, carry):
            @pl.when(z != sink)
            def _():
                chain_copy(d, c).wait_send()

            @pl.when(z != n - 1 - sink)
            def _():
                ahead_copy(d, c).wait_send()

            @pl.when((z == sink) & (lax.rem(c, width) != t))
            def _():
                scatter_copy(d, c, lax.rem(c, width), scatter_recv.at[0, 0]).wait_send()
                return_copy(d, c // width, lax.rem(c, width)).wait_send()

            return carry

        lax.fori_loop(0, half, settle, 0)
    final.wait()


def pick_kernel(group, index, in_ref, out_ref):
    base = pl.program_id(0) * group
    for k in range(group):
        out_ref[k] = in_ref[index[base + k]]


def fused(pieces, moments, owners):
    n = lax.axis_size("dp")
    width = lax.axis_size("tensor")
    me = lax.axis_index("dp")
    blocks_all, rows, columns = pieces.shape
    capacity = moments.shape[0]
    half = blocks_all // 2
    lead = min(2, half)
    slot_rank = ranks_of(owners)
    mine = owners == me
    ratio = decay_rate * decay_rate / (1.0 + decay_rate)
    weight = jnp.where(mine, ratio, 0.0).astype(jnp.float32)
    slot = jnp.minimum(slot_rank, capacity - 1)
    order = columns
    low = jnp.bfloat16
    all_results = pl.pallas_call(
        functools.partial(kernel, (n, width, half, rows, lead)),
        out_shape=jax.ShapeDtypeStruct((blocks_all, rows, columns), low),
        in_specs=[
            pl.BlockSpec(memory_space=pltpu.SMEM),
            pl.BlockSpec(memory_space=pltpu.SMEM),
            pl.BlockSpec(memory_space=pltpu.VMEM),
            pl.BlockSpec(memory_space=pltpu.VMEM),
        ],
        out_specs=pl.BlockSpec(memory_space=pl.ANY),
        scratch_shapes=[
            pltpu.VMEM((2, half, rows, columns), low),
            pltpu.VMEM((2, half, rows, columns), low),
            pltpu.VMEM((half // width, order, columns), low),
            pltpu.VMEM((half // width, order, columns), low),
            pltpu.VMEM((blocks_all, rows, columns), low),
            pltpu.VMEM((order, columns), jnp.float32),
            pltpu.SemaphoreType.DMA((2, half)),
            pltpu.SemaphoreType.DMA((2, half)),
            pltpu.SemaphoreType.DMA((half,)),
            pltpu.SemaphoreType.DMA((half // width, width)),
            pltpu.SemaphoreType.DMA((half // width, width)),
            pltpu.SemaphoreType.DMA((blocks_all,)),
            pltpu.SemaphoreType.DMA((blocks_all,)),
            pltpu.SemaphoreType.DMA,
        ],
        compiler_params=pltpu.CompilerParams(
            collective_id=0, has_side_effects=True, vmem_limit_bytes=50 * 1024 * 1024
        ),
        name="muon_chain",
    )(weight, slot, pieces, moments)

    slot_ids = jnp.arange(capacity, dtype=jnp.int32)
    places = jnp.arange(blocks_all, dtype=jnp.int32)
    my_slots = mine[:, None] & (slot_rank[:, None] == slot_ids[None, :])
    index = jnp.sum(jnp.where(my_slots, places[:, None], 0), axis=0)
    index = jnp.pad(index, (0, blocks_all - capacity))
    group = math.gcd(blocks_all, 4)
    return pl.pallas_call(
        functools.partial(pick_kernel, group),
        out_shape=jax.ShapeDtypeStruct((blocks_all, rows, columns), low),
        grid_spec=pltpu.PrefetchScalarGridSpec(
            num_scalar_prefetch=1,
            grid=(blocks_all // group,),
            in_specs=[pl.BlockSpec(memory_space=pltpu.VMEM)],
            out_specs=pl.BlockSpec((group, rows, columns), lambda s, index: (s, 0, 0)),
        ),
        name="muon_pick",
    )(index, all_results)


class Plan:
    def __init__(self, n, width, blocks_all, capacity, spare, place):
        self.n, self.width, self.place = n, width, place
        full, others = capacity, blocks_all - capacity
        some = others - spare
        self.full, self.others, self.some, self.spare = full, others, some, spare
        self.items = full + some
        last = n - 1
        if place == 0:
            self.shift = (0, spare - full)
            self.segments = (
                ((0, full, 0), (full, full + some, 1)),
                ((full - spare, full + some, last),),
            )
            self.ranges = ((0, full), (full, full + some), (full - spare, full + some))
        else:
            self.shift = (0, 0)
            self.segments = (
                ((0, some, 0), (some, some + full, place)),
                ((0, some, last), (some, some + full, place)),
            )
            self.ranges = ((0, some), (spare, some), (0, some))

    def positions(self):
        low, high = [], []
        for e in range(self.items):
            if self.place == 0:
                low.append(e)
                high.append(self.full + e if e < self.full else e)
            else:
                low.append(self.full + e if e < self.some else e - self.some)
                high.append(self.full + self.some + e if e < self.spare else low[-1])
        return low, high

    def candidates(self, f):
        first, end = self.ranges[1]
        first = jnp.where(f == 0, self.ranges[0][0], jnp.where(f == self.n - 1, self.ranges[2][0], first))
        end = jnp.where(f == 0, self.ranges[0][1], jnp.where(f == self.n - 1, self.ranges[2][1], end))
        if self.place > 0:
            first = jnp.where(f == self.place, self.some, first)
            end = jnp.where(f == self.place, self.items, end)
        return first, end

    def landing(self, f, e):
        if self.place == 0:
            return jnp.where((f > 0) & (e >= self.full), e - self.full, e)
        own = jnp.where(f == self.place, e - self.some, e)
        return jnp.where((f == self.n - 1) & (e < self.spare), e + self.some, own)


HOP = 2
SETTLE = 2
NS_TICKS = 2 * ITERS


def owner_kernel(
    plan, flip, rows, low_list, high_list, slots, weights, g_hbm, m_hbm, out_ref,
    g_ref, m_ref, arrived, partial, total, whole, ready, current, low_current, low_poly,
    load_sem, chain_send, chain_recv, scatter_send, scatter_recv, return_send, gather_recv,
):
    n, width, items = plan.n, plan.width, plan.items
    columns = g_ref.shape[2]
    z, t = lax.axis_index("dp"), lax.axis_index("tensor")
    f = n - 1 - z if flip else z
    step = (1, -1) if flip else (-1, 1)
    groups_most = whole.shape[0]
    low = jnp.bfloat16

    load_g = pltpu.make_async_copy(g_hbm, g_ref, load_sem.at[0])
    load_m = pltpu.make_async_copy(m_hbm, m_ref, load_sem.at[1])
    load_g.start()
    load_m.start()

    barrier = pltpu.get_barrier_semaphore()

    @pl.when(z > 0)
    def _():
        pl.semaphore_signal(barrier, inc=1, device_id=(z - 1, t), device_id_type=MESH)

    @pl.when(z < n - 1)
    def _():
        pl.semaphore_signal(barrier, inc=1, device_id=(z + 1, t), device_id_type=MESH)

    def greet(k, carry):
        peer = lax.rem(t + k, width)
        pl.semaphore_signal(barrier, inc=1, device_id=(z, peer), device_id_type=MESH)
        return carry

    lax.fori_loop(1, width, greet, 0)
    pl.semaphore_wait(barrier, jnp.where((z == 0) | (z == n - 1), width, width + 1))
    load_g.wait()
    load_m.wait()

    first, end = plan.candidates(f)
    groups = (end - first) // width
    lag_low = HOP * (n - 1 - f) + plan.shift[0]
    lag_high = HOP * f + plan.shift[1]
    lag = jnp.where(f == 0, lag_low, jnp.where(f == n - 1, lag_high, jnp.maximum(lag_low, lag_high)))

    def my_rows(place):
        return pl.ds(pl.multiple_of(place * rows, rows), rows)

    def chain_copy(d, e):
        return pltpu.make_async_remote_copy(
            src_ref=partial.at[d, e],
            dst_ref=arrived.at[d, e],
            send_sem=chain_send.at[d, e],
            recv_sem=chain_recv.at[d, e],
            device_id=(z + step[d], t),
            device_id_type=MESH,
        )

    def scatter_copy(u, peer):
        j = u // width
        return pltpu.make_async_remote_copy(
            src_ref=total.at[u],
            dst_ref=whole.at[j, my_rows(t)],
            send_sem=scatter_send.at[u],
            recv_sem=scatter_recv.at[j, t],
            device_id=(z, peer),
            device_id_type=MESH,
        )

    def return_copy(u, peer):
        j = u // width
        return pltpu.make_async_remote_copy(
            src_ref=ready.at[j, my_rows(peer)],
            dst_ref=out_ref.at[plan.landing(f, first + u)],
            send_sem=return_send.at[j, peer],
            recv_sem=gather_recv.at[u],
            device_id=(z, peer),
            device_id_type=MESH,
        )

    def takes_part(d, e):
        receives, sends = False, False
        for begin, stop, target in plan.segments[d]:
            inside = (e >= begin) & (e < stop)
            if d == 0:
                receives = receives | (inside & (f >= target) & (f < n - 1))
                sends = sends | (inside & (f > target))
            else:
                receives = receives | (inside & (f <= target) & (f > 0))
                sends = sends | (inside & (f < target))
        return receives, sends

    def flow(d, e):
        receives, sends = takes_part(d, e)
        blocks = low_list if d == 0 else high_list

        @pl.when(receives)
        def _():
            chain_copy(d, e).wait_recv()

        @pl.when(sends & receives)
        def _():
            mixed = g_ref[blocks[e]].astype(jnp.float32) + arrived[d, e].astype(jnp.float32)
            partial[d, e] = mixed.astype(low)

        @pl.when(sends & jnp.logical_not(receives))
        def _():
            partial[d, e] = g_ref[blocks[e]]

        @pl.when(sends)
        def _():
            chain_copy(d, e).start()

    def candidate(e):
        u = e - first

        def own(blocks):
            moment = m_ref[slots[e]].astype(jnp.float32)
            return g_ref[blocks[e]].astype(jnp.float32) + weights[e] * moment

        @pl.when(f == 0)
        def _():
            total[u] = (own(low_list) + arrived[0, e].astype(jnp.float32)).astype(low)

        @pl.when(f == n - 1)
        def _():
            total[u] = (own(high_list) + arrived[1, e].astype(jnp.float32)).astype(low)

        @pl.when((f > 0) & (f < n - 1))
        def _():
            both = arrived[0, e].astype(jnp.float32) + arrived[1, e].astype(jnp.float32)
            total[u] = (own(low_list) + both).astype(low)

        peer = lax.rem(u, width)

        @pl.when(peer == t)
        def _():
            whole[u // width, my_rows(t)] = total[u]

        @pl.when(peer != t)
        def _():
            scatter_copy(u, peer).start()

    def begin_block(j):
        def land(k, carry):
            peer = lax.rem(t + k, width)
            pltpu.make_async_copy(
                total.at[0], whole.at[j, my_rows(peer)], scatter_recv.at[j, peer]
            ).wait()
            return carry

        lax.fori_loop(1, width, land, 0)
        widened = whole[j].astype(jnp.float32) * (1.0 + decay_rate)
        length = jnp.sqrt(jnp.sum(widened * widened)) + norm_eps
        start = widened / length
        current[...] = start
        low_current[...] = start.astype(low)

    def make_polynomial():
        now = low_current[...]
        squared = lax.dot_general(now, now, (((1,), (1,)), ((), ())), preferred_element_type=jnp.float32)
        low_squared = squared.astype(low)
        polynomial = newton_b * squared + newton_c * jnp.dot(
            low_squared, low_squared, preferred_element_type=jnp.float32
        )
        low_poly[...] = polynomial.astype(low)

    def apply_polynomial():
        later = newton_a * current[...] + jnp.dot(
            low_poly[...], low_current[...], preferred_element_type=jnp.float32
        )
        current[...] = later
        low_current[...] = later.astype(low)

    def finish_block(j):
        ready[j] = (current[...] * math.sqrt(columns)).astype(low)
        u = j * width + t

        def give(k, carry):
            return_copy(u, lax.rem(t + k, width)).start()
            return carry

        pltpu.make_async_copy(
            ready.at[j, my_rows(t)], out_ref.at[plan.landing(f, first + u)], gather_recv.at[u]
        ).start()
        lax.fori_loop(1, width, give, 0)

    def tick(i, carry):
        flow(0, i - lag_low)
        flow(1, i - lag_high)
        e = i - lag

        @pl.when((e >= first) & (e < end))
        def _():
            candidate(e)

        since = e - first - t - SETTLE
        j, phase = since // width, lax.rem(since, width)
        active = (since >= 0) & (j < groups) & (phase < NS_TICKS)

        @pl.when(active & (phase == 0))
        def _():
            begin_block(j)

        @pl.when(active & (lax.rem(phase, 2) == 0))
        def _():
            make_polynomial()

        @pl.when(active & (lax.rem(phase, 2) == 1))
        def _():
            apply_polynomial()

        @pl.when(active & (phase == NS_TICKS - 1))
        def _():
            finish_block(j)

        return carry

    lax.fori_loop(0, items + HOP * (n - 1) + SETTLE + NS_TICKS, tick, 0)

    def settle(e, carry):
        for d in range(2):
            sends = takes_part(d, e)[1]

            @pl.when(sends)
            def _():
                chain_copy(d, e).wait_send()

        return carry

    lax.fori_loop(0, items, settle, 0)

    def collect(u, carry):
        @pl.when(u < groups * width)
        def _():
            peer = lax.rem(u, width)

            @pl.when(peer != t)
            def _():
                scatter_copy(u, peer).wait_send()
                return_copy(u - peer + t, peer).wait_send()

            pltpu.make_async_copy(
                total.at[0], out_ref.at[plan.landing(f, first + u)], gather_recv.at[u]
            ).wait()

        return carry

    lax.fori_loop(0, groups_most * width, collect, 0)


def by_owner(plan, flip, ident, low_list, high_list, slots, weights, pieces, moments):
    blocks_all, rows, columns = pieces.shape
    width, items = plan.width, plan.items
    groups = max(end - begin for begin, end in plan.ranges + ((0, plan.full),)) // width
    low = jnp.bfloat16
    return pl.pallas_call(
        functools.partial(owner_kernel, plan, flip, rows),
        out_shape=jax.ShapeDtypeStruct((blocks_all, rows, columns), low),
        in_specs=[pl.BlockSpec(memory_space=pltpu.SMEM)] * 4 + [pl.BlockSpec(memory_space=pl.ANY)] * 2,
        out_specs=pl.BlockSpec(memory_space=pl.ANY),
        scratch_shapes=[
            pltpu.VMEM(pieces.shape, low),
            pltpu.VMEM(moments.shape, low),
            pltpu.VMEM((2, items, rows, columns), low),
            pltpu.VMEM((2, items, rows, columns), low),
            pltpu.VMEM((groups * width, rows, columns), low),
            pltpu.VMEM((groups, columns, columns), low),
            pltpu.VMEM((groups, columns, columns), low),
            pltpu.VMEM((columns, columns), jnp.float32),
            pltpu.VMEM((columns, columns), low),
            pltpu.VMEM((columns, columns), low),
            pltpu.SemaphoreType.DMA((2,)),
            pltpu.SemaphoreType.DMA((2, items)),
            pltpu.SemaphoreType.DMA((2, items)),
            pltpu.SemaphoreType.DMA((groups * width,)),
            pltpu.SemaphoreType.DMA((groups, width)),
            pltpu.SemaphoreType.DMA((groups, width)),
            pltpu.SemaphoreType.DMA((groups * width,)),
        ],
        compiler_params=pltpu.CompilerParams(
            collective_id=ident, has_side_effects=True, vmem_limit_bytes=50 * 1024 * 1024
        ),
        name=f"muon_owner_{ident}",
    )(low_list, high_list, slots, weights, pieces, moments)


def routed(gradients, momentum, owners):
    n, width = lax.axis_size("dp"), lax.axis_size("tensor")
    me = lax.axis_index("dp")
    pieces, moments = gradients[0], momentum[0]
    blocks_all, rows, columns = pieces.shape
    capacity = moments.shape[0]
    spare = width
    last = n - 1
    plans = [Plan(n, width, blocks_all, capacity, spare, min(p, last - p)) for p in range(n)]

    groups = jnp.arange(n, dtype=jnp.int32)
    places = jnp.arange(blocks_all, dtype=jnp.int32)
    counts = jnp.sum((owners[:, None] == groups[None, :]).astype(jnp.int32), axis=0)
    fullest = jnp.max(jnp.where(counts == capacity, groups, 0))
    flip = fullest > last - fullest
    along = jnp.where(flip, last - owners, owners)
    key = jnp.where(owners == fullest, -1, along)
    before = (key[None, :] < key[:, None]) | ((key[None, :] == key[:, None]) & (places[None, :] < places[:, None]))
    position = jnp.sum(before.astype(jnp.int32), axis=1)

    my_along = jnp.where(flip, last - me, me)
    my_key = jnp.where(me == fullest, -1, my_along)
    begin = jnp.sum((key < my_key).astype(jnp.int32))
    count = jnp.sum((owners == me).astype(jnp.int32))
    maps = [jnp.array(plan.positions(), jnp.int32) for plan in plans[: (n + 1) // 2]]
    turn = jnp.minimum(fullest, last - fullest)
    wanted = maps[0]
    for k in range(1, len(maps)):
        wanted = jnp.where(turn == k, maps[k], wanted)
    lists = jnp.sum(jnp.where(position[None, None, :] == wanted[:, :, None], places[None, None, :], 0), axis=2)
    here = jnp.where(my_along == last, wanted[1], wanted[0])
    slots = jnp.clip(here - begin, 0, capacity - 1)
    weights = jnp.where(
        (here >= begin) & (here < begin + count), decay_rate * decay_rate / (1.0 + decay_rate), 0.0
    ).astype(jnp.float32)

    ends = (counts[0] >= spare) & (counts[last] >= spare)
    branch = jnp.where(ends, fullest, n)
    branches = [
        functools.partial(by_owner, plans[p], p > last - p, p + 1) for p in range(n)
    ]
    branches.append(lambda a, b, c, d, g, m: fused(g, m, owners))
    found = lax.switch(branch, branches, lists[0], lists[1], slots, weights, pieces, moments)
    offset = jnp.where(ends & (me != fullest), begin - capacity, 0)
    chosen = lax.dynamic_slice_in_dim(found, offset, capacity, axis=0)
    filled = jnp.arange(capacity, dtype=jnp.int32) < count
    return jnp.where(filled[:, None, None], chosen.astype(jnp.float32), 0.0)[None]


def choose(gradients, momentum, owners):
    n, width = lax.axis_size("dp"), lax.axis_size("tensor")
    blocks_all, rows = gradients.shape[1:3]
    capacity = momentum.shape[1]
    others = blocks_all - capacity
    even = blocks_all % (2 * width) == 0 and capacity % width == 0 and others % width == 0
    if n == 4 and even and width < others <= capacity and rows % 16 == 0 and width >= NS_TICKS:
        return routed(gradients, momentum, owners)
    return body(gradients, momentum, owners)


def solution(mesh):
    in_specs = (P("dp", None, "tensor", None), P("dp", None, "tensor", None), P())
    out_specs = P("dp", None, "tensor", None)
    return jax.shard_map(choose, mesh=mesh, in_specs=in_specs, out_specs=out_specs, check_vma=False)
```

```python
import functools
import math

import jax
import jax.numpy as jnp
from jax import lax
from jax.experimental import pallas as pl
from jax.experimental.pallas import tpu as pltpu
from jax.sharding import PartitionSpec as P

ITERS = 3


decay_rate = 0.95
newton_a = 3.4445
newton_b = -4.775
newton_c = 2.0315
norm_eps = 1e-07


def ranks_of(labels):
    length = labels.shape[0]
    places = jnp.arange(length, dtype=jnp.int32)
    earlier = (labels[None, :] == labels[:, None]) & (places[None, :] < places[:, None])
    return jnp.sum(earlier.astype(jnp.int32), axis=1)


def rows_at(array, index):
    count = array.shape[0]
    chosen = (index[:, None] == jnp.arange(count, dtype=jnp.int32)[None, :]).astype(array.dtype)
    picked = jnp.dot(chosen, array.reshape(count, -1), preferred_element_type=jnp.float32)
    return picked.astype(array.dtype).reshape((index.shape[0],) + array.shape[1:])


def dot(spec, left, right):
    return jnp.einsum(
        spec,
        left.astype(jnp.bfloat16),
        right.astype(jnp.bfloat16),
        preferred_element_type=jnp.float32,
    )


def iterate(blocks):
    widened = blocks.astype(jnp.float32) * (1.0 + decay_rate)
    lengths = jnp.sqrt(jnp.sum(widened * widened, axis=(1, 2), keepdims=True)) + norm_eps
    current = widened / lengths
    scale_up = math.sqrt(blocks.shape[1])
    for iteration in range(ITERS):
        squared = dot("kij,klj->kil", current, current)
        polynomial = newton_b * squared + newton_c * dot("kij,kjl->kil", squared, squared)
        current = newton_a * current + dot("kij,kjl->kil", polynomial, current)
    return current * scale_up


def body(gradients, momentum, owners):
    dp_count = lax.axis_size("dp")
    tp_count = lax.axis_size("tensor")
    my_group = lax.axis_index("dp")
    pieces = gradients[0]
    blocks_all, rows, columns = pieces.shape
    per_group = blocks_all // dp_count
    capacity = momentum.shape[1]
    slot_rank = ranks_of(owners)
    places = jnp.arange(blocks_all, dtype=jnp.int32)

    mine = owners == my_group
    moment = rows_at(momentum[0], jnp.minimum(slot_rank, capacity - 1))
    moment = jnp.where(mine[:, None, None], moment, jnp.zeros_like(moment)).astype(jnp.float32)
    ratio = decay_rate * decay_rate / (1.0 + decay_rate)
    folded = (pieces.astype(jnp.float32) + ratio * moment).astype(jnp.bfloat16)
    held = lax.psum_scatter(folded, "dp", scatter_dimension=0, tiled=True)

    per_device = (per_group + tp_count - 1) // tp_count
    padded_count = per_device * tp_count
    padded = jnp.pad(held, ((0, padded_count - per_group), (0, 0), (0, 0)))
    whole = lax.all_to_all(padded, "tensor", split_axis=0, concat_axis=1, tiled=True)
    finished = iterate(whole).astype(jnp.bfloat16)
    result = lax.all_to_all(finished, "tensor", split_axis=1, concat_axis=0, tiled=True)

    groups = jnp.arange(dp_count, dtype=jnp.int32)
    pair_most = (2 * per_group + dp_count - 1) // dp_count
    held_owner = lax.dynamic_slice_in_dim(owners, my_group * per_group, per_group)
    held_rank = ranks_of(held_owner)
    held_places = jnp.arange(per_group, dtype=jnp.int32)
    pair_ids = jnp.arange(pair_most, dtype=jnp.int32)
    matched = (held_owner[:, None, None] == groups[None, :, None]) & (
        held_rank[:, None, None] == pair_ids[None, None, :]
    )
    source = jnp.sum(jnp.where(matched, held_places[:, None, None], 0), axis=0).reshape(-1)
    outgoing = rows_at(result, source)
    outgoing = outgoing.reshape(dp_count, pair_most, rows, columns)
    incoming = lax.all_to_all(outgoing, "dp", split_axis=0, concat_axis=0, tiled=True)
    incoming = incoming.reshape(dp_count * pair_most, rows, columns)
    group_rank = ranks_of(owners * dp_count + places // per_group)
    position = places // per_group * pair_most + group_rank
    slot_ids = jnp.arange(capacity, dtype=jnp.int32)
    my_slots = mine[:, None] & (slot_rank[:, None] == slot_ids[None, :])
    occupied = jnp.any(my_slots, axis=0)
    arriving = jnp.sum(jnp.where(my_slots, position[:, None], 0), axis=0)
    chosen = rows_at(incoming, arriving).astype(jnp.float32)
    update = jnp.where(occupied[:, None, None], chosen, jnp.zeros_like(chosen))
    return update[None]


MESH = pl.DeviceIdType.MESH


def kernel(
    sizes, weight, slot, g_ref, m_ref, out_ref,
    arrived, partial, whole, ready, gathered, current,
    chain_send, chain_recv, scatter_send, scatter_recv, return_send, ahead_send, gather_recv, out_sem,
):
    n, width, half, rows, lead = sizes
    columns = g_ref.shape[2]
    z, t = lax.axis_index("dp"), lax.axis_index("tensor")
    per_device = half // width
    gap = half
    is_end = (z == 0) | (z == n - 1)
    low = 2 * z < n - 1

    barrier = pltpu.get_barrier_semaphore()

    @pl.when(z > 0)
    def _():
        pl.semaphore_signal(barrier, inc=1, device_id=(z - 1, t), device_id_type=MESH)

    @pl.when(z < n - 1)
    def _():
        pl.semaphore_signal(barrier, inc=1, device_id=(z + 1, t), device_id_type=MESH)

    def greet(k, carry):
        peer = lax.rem(t + k, width)
        pl.semaphore_signal(barrier, inc=1, device_id=(z, peer), device_id_type=MESH)
        return carry

    lax.fori_loop(1, width, greet, 0)
    pl.semaphore_wait(barrier, jnp.where(is_end, width, width + 1))

    def chain_copy(d, c):
        return pltpu.make_async_remote_copy(
            src_ref=partial.at[d, c],
            dst_ref=arrived.at[d, c],
            send_sem=chain_send.at[d, c],
            recv_sem=chain_recv.at[d, c],
            device_id=(z + 2 * d - 1, t),
            device_id_type=MESH,
        )

    def own(d, c):
        block = d * half + c
        moment = m_ref[slot[block]].astype(jnp.float32)
        return g_ref[block].astype(jnp.float32) + weight[block] * moment

    def my_rows(place):
        return pl.ds(pl.multiple_of(place * rows, rows), rows)

    def start_chain(d, c):
        partial[d, c] = own(d, c).astype(jnp.bfloat16)
        chain_copy(d, c).start()

    def add_chain(d, c):
        chain_copy(d, c).wait_recv()
        total = own(d, c) + arrived[d, c].astype(jnp.float32)
        partial[d, c] = total.astype(jnp.bfloat16)

    def scatter_copy(d, c, peer, sem):
        return pltpu.make_async_remote_copy(
            src_ref=partial.at[d, c],
            dst_ref=whole.at[c // width, my_rows(t)],
            send_sem=scatter_send.at[c],
            recv_sem=sem,
            device_id=(z, peer),
            device_id_type=MESH,
        )

    def return_copy(d, j, peer):
        block = d * half + j * width + t
        return pltpu.make_async_remote_copy(
            src_ref=ready.at[j, my_rows(peer)],
            dst_ref=gathered.at[block],
            send_sem=return_send.at[j, peer],
            recv_sem=gather_recv.at[block],
            device_id=(z, peer),
            device_id_type=MESH,
        )

    def ahead_copy(d, c):
        block = d * half + c
        return pltpu.make_async_remote_copy(
            src_ref=gathered.at[block],
            dst_ref=gathered.at[block],
            send_sem=ahead_send.at[block],
            recv_sem=gather_recv.at[block],
            device_id=(z + 1 - 2 * d, t),
            device_id_type=MESH,
        )

    def pass_on(d, c):
        ahead_copy(d, c).wait_recv()

        @pl.when((z + 1 - 2 * d >= 0) & (z + 1 - 2 * d < n))
        def _():
            ahead_copy(d, c).start()

    def iterate_in(j):
        widened = whole[j].astype(jnp.float32) * (1.0 + decay_rate)
        length = jnp.sqrt(jnp.sum(widened * widened)) + norm_eps
        current[...] = widened / length

        def once(k, carry):
            now = current[...]
            low_now = now.astype(jnp.bfloat16)
            squared = lax.dot_general(
                low_now, low_now, (((1,), (1,)), ((), ())), preferred_element_type=jnp.float32
            )
            low_squared = squared.astype(jnp.bfloat16)
            polynomial = newton_b * squared + newton_c * jnp.dot(
                low_squared, low_squared, preferred_element_type=jnp.float32
            )
            current[...] = newton_a * now + jnp.dot(
                polynomial.astype(jnp.bfloat16), low_now, preferred_element_type=jnp.float32
            )
            return carry

        lax.fori_loop(0, ITERS, once, 0)
        ready[j] = (current[...] * math.sqrt(columns)).astype(jnp.bfloat16)

    @pl.when(is_end)
    def _():
        near = jnp.where(z == 0, 0, 1)
        far = 1 - near

        def begin(c, carry):
            start_chain(far, c)
            return carry

        lax.fori_loop(0, half, begin, 0)

        def pass_group(j):
            def one(k, inner):
                pass_on(near, j * width + k)
                return inner

            lax.fori_loop(0, width, one, 0)

        def reduce_group(j):
            def chunk(k, inner):
                c = j * width + k
                add_chain(near, c)

                @pl.when(k == t)
                def _():
                    pltpu.make_async_copy(
                        partial.at[near, c], whole.at[j, my_rows(t)], scatter_recv.at[j, t]
                    ).start()

                @pl.when(k != t)
                def _():
                    scatter_copy(near, c, k, scatter_recv.at[j, t]).start()

                return inner

            lax.fori_loop(0, width, chunk, 0)

        def iterate_group(j):
            def land(k, inner):
                pltpu.make_async_copy(
                    partial.at[near, 0], whole.at[j, my_rows(k)], scatter_recv.at[j, k]
                ).wait()
                return inner

            lax.fori_loop(0, width, land, 0)
            iterate_in(j)

            def give(k, inner):
                @pl.when(k == t)
                def _():
                    block = near * half + j * width + t
                    pltpu.make_async_copy(
                        ready.at[j, my_rows(t)], gathered.at[block], gather_recv.at[block]
                    ).start()

                @pl.when(k != t)
                def _():
                    return_copy(near, j, k).start()

                return inner

            lax.fori_loop(0, width, give, 0)

        def block_step(j, carry):
            @pl.when(j < per_device)
            def _():
                reduce_group(j)

            @pl.when(j > 1)
            def _():
                pass_group(j - 2)

            @pl.when(j > 0)
            def _():
                iterate_group(j - 1)

            return carry

        lax.fori_loop(0, per_device + 1, block_step, 0)
        pass_group(per_device - 1)

        def finish(c, carry):
            pass_on(far, c)
            return carry

        lax.fori_loop(0, half, finish, 0)

    @pl.when(jnp.logical_not(is_end))
    def _():
        early = jnp.where(low, 1, 0)

        def forward(d, c):
            add_chain(d, c)
            chain_copy(d, c).start()

        def step(i, carry):
            @pl.when(i < half)
            def _():
                forward(early, i)

            @pl.when((i >= lead) & (i < half + lead))
            def _():
                forward(1 - early, i - lead)

            @pl.when((i >= gap) & (i < half + gap))
            def _():
                pass_on(1 - early, i - gap)

            @pl.when(i >= gap + lead)
            def _():
                pass_on(early, i - gap - lead)

            return carry

        lax.fori_loop(0, half + gap + lead, step, 0)

    final = pltpu.make_async_copy(gathered, out_ref, out_sem)
    final.start()

    for d in range(2):
        sink = 0 if d == 0 else n - 1

        def settle(c, carry):
            @pl.when(z != sink)
            def _():
                chain_copy(d, c).wait_send()

            @pl.when(z != n - 1 - sink)
            def _():
                ahead_copy(d, c).wait_send()

            @pl.when((z == sink) & (lax.rem(c, width) != t))
            def _():
                scatter_copy(d, c, lax.rem(c, width), scatter_recv.at[0, 0]).wait_send()
                return_copy(d, c // width, lax.rem(c, width)).wait_send()

            return carry

        lax.fori_loop(0, half, settle, 0)
    final.wait()


def pick_kernel(group, index, in_ref, out_ref):
    base = pl.program_id(0) * group
    for k in range(group):
        out_ref[k] = in_ref[index[base + k]]


def fused(pieces, moments, owners):
    n = lax.axis_size("dp")
    width = lax.axis_size("tensor")
    me = lax.axis_index("dp")
    blocks_all, rows, columns = pieces.shape
    capacity = moments.shape[0]
    half = blocks_all // 2
    lead = min(2, half)
    slot_rank = ranks_of(owners)
    mine = owners == me
    ratio = decay_rate * decay_rate / (1.0 + decay_rate)
    weight = jnp.where(mine, ratio, 0.0).astype(jnp.float32)
    slot = jnp.minimum(slot_rank, capacity - 1)
    order = columns
    low = jnp.bfloat16
    all_results = pl.pallas_call(
        functools.partial(kernel, (n, width, half, rows, lead)),
        out_shape=jax.ShapeDtypeStruct((blocks_all, rows, columns), low),
        in_specs=[
            pl.BlockSpec(memory_space=pltpu.SMEM),
            pl.BlockSpec(memory_space=pltpu.SMEM),
            pl.BlockSpec(memory_space=pltpu.VMEM),
            pl.BlockSpec(memory_space=pltpu.VMEM),
        ],
        out_specs=pl.BlockSpec(memory_space=pl.ANY),
        scratch_shapes=[
            pltpu.VMEM((2, half, rows, columns), low),
            pltpu.VMEM((2, half, rows, columns), low),
            pltpu.VMEM((half // width, order, columns), low),
            pltpu.VMEM((half // width, order, columns), low),
            pltpu.VMEM((blocks_all, rows, columns), low),
            pltpu.VMEM((order, columns), jnp.float32),
            pltpu.SemaphoreType.DMA((2, half)),
            pltpu.SemaphoreType.DMA((2, half)),
            pltpu.SemaphoreType.DMA((half,)),
            pltpu.SemaphoreType.DMA((half // width, width)),
            pltpu.SemaphoreType.DMA((half // width, width)),
            pltpu.SemaphoreType.DMA((blocks_all,)),
            pltpu.SemaphoreType.DMA((blocks_all,)),
            pltpu.SemaphoreType.DMA,
        ],
        compiler_params=pltpu.CompilerParams(
            collective_id=0, has_side_effects=True, vmem_limit_bytes=50 * 1024 * 1024
        ),
        name="muon_chain",
    )(weight, slot, pieces, moments)

    slot_ids = jnp.arange(capacity, dtype=jnp.int32)
    places = jnp.arange(blocks_all, dtype=jnp.int32)
    my_slots = mine[:, None] & (slot_rank[:, None] == slot_ids[None, :])
    index = jnp.sum(jnp.where(my_slots, places[:, None], 0), axis=0)
    index = jnp.pad(index, (0, blocks_all - capacity))
    group = math.gcd(blocks_all, 4)
    return pl.pallas_call(
        functools.partial(pick_kernel, group),
        out_shape=jax.ShapeDtypeStruct((blocks_all, rows, columns), low),
        grid_spec=pltpu.PrefetchScalarGridSpec(
            num_scalar_prefetch=1,
            grid=(blocks_all // group,),
            in_specs=[pl.BlockSpec(memory_space=pltpu.VMEM)],
            out_specs=pl.BlockSpec((group, rows, columns), lambda s, index: (s, 0, 0)),
        ),
        name="muon_pick",
    )(index, all_results)


AHEAD = 6
HOP = 3
SETTLE = 4
NS_TICKS = 2 * ITERS


def over(scaled, divisor):
    if isinstance(scaled, int):
        return scaled // divisor
    return (scaled * ((1 << 18) // divisor + 1)) >> 18


def at_most(limit, value):
    return min(limit, value) if isinstance(value, int) and isinstance(limit, int) else jnp.minimum(limit, value)


def pick(condition, yes, no):
    return (yes if condition else no) if isinstance(condition, bool) else jnp.where(condition, yes, no)


class Plan:
    def __init__(self, n, width, blocks_all, capacity, spare, place):
        self.n, self.width, self.place, self.last = n, width, place, n - 1
        self.full, self.spare = capacity, spare
        self.some = blocks_all - capacity - spare
        self.items = self.full + self.some
        self.batch = self.some // spare
        self.early = HOP - 1 if place == 0 else 0

    def firsts(self, e):
        if self.place == 0:
            span = self.items - self.early
            return at_most(self.full, over(e * self.full + span - 1, span))
        return over(e * self.full, self.items)

    def split(self, e):
        p = self.firsts(e)
        return self.firsts(e + 1) > p, p, e - p

    def item(self, first_kind, u):
        full, some, items, early = self.full, self.some, self.items, self.early
        if self.place == 0:
            span, rest = items - early, some - early
            first = over(u * span, full)
            other = at_most(over((u + 1) * span + rest - 1, rest) - 1, full + u)
        else:
            first = over((u + 1) * items + full - 1, full) - 1
            other = over(u * items, some)
        return jnp.where(first_kind, first, other)

    def shuffled(self, r):
        group = over(r, self.batch + 1)
        k = r - group * (self.batch + 1)
        return pick(k == self.batch, self.some + group, group * self.batch + k)

    def positions(self):
        low, high = [], []
        for e in range(self.items):
            is_first, p, q = self.split(e)
            low.append(p if is_first else self.full + q)
            if self.place == 0:
                high.append(self.full + min(self.shuffled(p), self.some + self.spare - 1))
            else:
                high.append(p if is_first else self.full + (self.some + q if q < self.spare else q))
        return low, high

    def targets(self, d, is_first):
        if self.place == 0:
            return jnp.where(is_first, 0, 1) if d == 0 else self.last
        return jnp.where(is_first, self.place, 0 if d == 0 else self.last)

    def carried(self, d, is_first):
        return is_first if self.place == 0 and d == 1 else True

    def works_on_firsts(self, f):
        return (f == 0) | (f == self.last) if self.place == 0 else f == self.place

    def skipped(self, f):
        if self.place == 0:
            return 0
        return jnp.where((f == 0) | (f == self.last) | (f == self.place), 0, self.spare)

    def landing(self, f, u):
        if self.place == 0:
            return jnp.where(f == self.last, self.shuffled(u), u)
        q = u + self.skipped(f)
        return jnp.where((f == self.last) & (q < self.spare), q + self.some, q)

    def other_item(self, e, q):
        if self.place == 0:
            return self.item(True, q + over(q, self.batch))
        return e


def owner_kernel(
    plan, flip, rows, table, g_hbm, m_hbm, out_ref,
    g_ref, m_ref, arrived, partial, total, whole, ready, current, low_current, low_poly,
    load_sem, chain_send, chain_recv, scatter_send, scatter_recv, return_send, gather_recv,
):
    n, width, items = plan.n, plan.width, plan.items
    columns = g_ref.shape[2]
    z, t = lax.axis_index("dp"), lax.axis_index("tensor")
    f = n - 1 - z if flip else z
    step = (1, -1) if flip else (-1, 1)
    groups_most = whole.shape[0]
    low = jnp.bfloat16

    load_g = pltpu.make_async_copy(g_hbm, g_ref, load_sem.at[0])
    load_m = pltpu.make_async_copy(m_hbm, m_ref, load_sem.at[1])
    load_g.start()
    load_m.start()

    barrier = pltpu.get_barrier_semaphore()

    @pl.when(z > 0)
    def _():
        pl.semaphore_signal(barrier, inc=1, device_id=(z - 1, t), device_id_type=MESH)

    @pl.when(z < n - 1)
    def _():
        pl.semaphore_signal(barrier, inc=1, device_id=(z + 1, t), device_id_type=MESH)

    def greet(k, carry):
        peer = lax.rem(t + k, width)
        pl.semaphore_signal(barrier, inc=1, device_id=(z, peer), device_id_type=MESH)
        return carry

    lax.fori_loop(1, width, greet, 0)
    pl.semaphore_wait(barrier, jnp.where((z == 0) | (z == n - 1), width, width + 1))
    load_g.wait()
    load_m.wait()

    on_firsts = plan.works_on_firsts(f)
    skipped = plan.skipped(f)
    count = jnp.where(on_firsts, plan.full, plan.some - skipped)
    groups = count // width
    lag_low = HOP * (n - 1 - f)
    lag_high = HOP * f
    lag = jnp.where(f == 0, lag_low, jnp.where(f == n - 1, lag_high, jnp.maximum(lag_low, lag_high)))

    def my_rows(place):
        return pl.ds(pl.multiple_of(place * rows, rows), rows)

    spread = width // 2
    my_turn = t // 2 + lax.rem(t, 2) * spread

    def peer_of(u):
        k = lax.rem(u, width)
        return lax.rem(k, spread) * 2 + k // spread

    def chain_copy(d, e):
        return pltpu.make_async_remote_copy(
            src_ref=partial.at[d, e],
            dst_ref=arrived.at[d, e],
            send_sem=chain_send.at[d, e],
            recv_sem=chain_recv.at[d, e],
            device_id=(z + step[d], t),
            device_id_type=MESH,
        )

    def scatter_copy(u, peer):
        j = u // width
        return pltpu.make_async_remote_copy(
            src_ref=total.at[u],
            dst_ref=whole.at[j, my_rows(t)],
            send_sem=scatter_send.at[u],
            recv_sem=scatter_recv.at[j, t],
            device_id=(z, peer),
            device_id_type=MESH,
        )

    def return_copy(u, peer):
        j = u // width
        return pltpu.make_async_remote_copy(
            src_ref=ready.at[j, my_rows(peer)],
            dst_ref=out_ref.at[plan.landing(f, u)],
            send_sem=return_send.at[j, peer],
            recv_sem=gather_recv.at[u],
            device_id=(z, peer),
            device_id_type=MESH,
        )

    def takes_part(d, e):
        is_first = plan.split(e)[0]
        target = plan.targets(d, is_first)
        inside = (e >= 0) & (e < items) & plan.carried(d, is_first)
        if d == 0:
            return inside & (f >= target) & (f < n - 1), inside & (f > target)
        return inside & (f <= target) & (f > 0), inside & (f < target)

    def flow(d, e):
        receives, sends = takes_part(d, e)
        blocks = d * items + e

        @pl.when(receives)
        def _():
            chain_copy(d, e).wait_recv()

        @pl.when(sends & receives)
        def _():
            mixed = g_ref[table[blocks]].astype(jnp.float32) + arrived[d, e].astype(jnp.float32)
            partial[d, e] = mixed.astype(low)

        @pl.when(sends & jnp.logical_not(receives))
        def _():
            partial[d, e] = g_ref[table[blocks]]

        @pl.when(sends)
        def _():
            chain_copy(d, e).start()

    def candidate(e, u):
        def own(d):
            weight = table[3 * items + e].astype(jnp.float32) * (decay_rate * decay_rate / (1.0 + decay_rate))
            moment = m_ref[table[2 * items + e]].astype(jnp.float32)
            return g_ref[table[d * items + e]].astype(jnp.float32) + weight * moment

        @pl.when(f == 0)
        def _():
            total[u] = (own(0) + arrived[0, e].astype(jnp.float32)).astype(low)

        @pl.when(f == n - 1)
        def _():
            total[u] = (own(1) + arrived[1, e].astype(jnp.float32)).astype(low)

        @pl.when((f > 0) & (f < n - 1))
        def _():
            twin = plan.other_item(e, u + skipped)
            both = arrived[0, e].astype(jnp.float32) + arrived[1, twin].astype(jnp.float32)
            total[u] = (own(0) + both).astype(low)

        peer = peer_of(u)

        @pl.when(peer == t)
        def _():
            whole[u // width, my_rows(t)] = total[u]

        @pl.when(peer != t)
        def _():
            scatter_copy(u, peer).start()

    def begin_block(j):
        def land(k, carry):
            peer = lax.rem(t + k, width)
            pltpu.make_async_copy(
                total.at[0], whole.at[j, my_rows(peer)], scatter_recv.at[j, peer]
            ).wait()
            return carry

        lax.fori_loop(1, width, land, 0)
        widened = whole[j].astype(jnp.float32) * (1.0 + decay_rate)
        length = jnp.sqrt(jnp.sum(widened * widened)) + norm_eps
        start = widened / length
        current[...] = start
        low_current[...] = start.astype(low)

    def make_polynomial():
        now = low_current[...]
        squared = lax.dot_general(now, now, (((1,), (1,)), ((), ())), preferred_element_type=jnp.float32)
        low_squared = squared.astype(low)
        polynomial = newton_b * squared + newton_c * jnp.dot(
            low_squared, low_squared, preferred_element_type=jnp.float32
        )
        low_poly[...] = polynomial.astype(low)

    def apply_polynomial():
        later = newton_a * current[...] + jnp.dot(
            low_poly[...], low_current[...], preferred_element_type=jnp.float32
        )
        current[...] = later
        low_current[...] = later.astype(low)

    def finish_block(j):
        ready[j] = (current[...] * math.sqrt(columns)).astype(low)
        u = j * width + my_turn

        def give(k, carry):
            return_copy(u, lax.rem(t + k, width)).start()
            return carry

        pltpu.make_async_copy(
            ready.at[j, my_rows(t)], out_ref.at[plan.landing(f, u)], gather_recv.at[u]
        ).start()
        lax.fori_loop(1, width, give, 0)

    def tick(moment, carry):
        i = moment - AHEAD
        flow(0, i - lag_low + jnp.where(f == n - 1, AHEAD, 0))
        flow(1, i - lag_high + jnp.where(f == 0, AHEAD, 0))
        e = i - lag
        is_first, p, q = plan.split(e)
        u = jnp.where(on_firsts, p, q - skipped)

        @pl.when((is_first == on_firsts) & (e >= 0) & (e < items) & (u >= 0))
        def _():
            candidate(e, u)

        since = jnp.maximum(e - SETTLE, -1)
        firsts = plan.firsts(since + 1)
        known = jnp.minimum(jnp.where(on_firsts, firsts, since + 1 - firsts - skipped), count)
        j = jnp.maximum(known - 1 - my_turn, 0) // width
        phase = since - plan.item(on_firsts, j * width + my_turn + jnp.where(on_firsts, 0, skipped))
        active = (known > my_turn) & (phase < NS_TICKS)

        @pl.when(active & (phase == 0))
        def _():
            begin_block(j)

        @pl.when(active & (phase % 2 == 0))
        def _():
            make_polynomial()

        @pl.when(active & (phase % 2 == 1))
        def _():
            apply_polynomial()

        @pl.when(active & (phase == NS_TICKS - 1))
        def _():
            finish_block(j)

        return carry

    lax.fori_loop(0, AHEAD + items + HOP * (n - 1) + SETTLE + NS_TICKS, tick, 0)

    def settle(e, carry):
        for d in range(2):
            sends = takes_part(d, e)[1]

            @pl.when(sends)
            def _():
                chain_copy(d, e).wait_send()

        return carry

    lax.fori_loop(0, items, settle, 0)

    def collect(u, carry):
        @pl.when(u < groups * width)
        def _():
            peer = peer_of(u)

            @pl.when(peer != t)
            def _():
                scatter_copy(u, peer).wait_send()
                return_copy(u, peer).wait_send()

            pltpu.make_async_copy(
                total.at[0], out_ref.at[plan.landing(f, u)], gather_recv.at[u]
            ).wait()

        return carry

    lax.fori_loop(0, groups_most * width, collect, 0)


def by_owner(plan, flip, ident, table, pieces, moments):
    blocks_all, rows, columns = pieces.shape
    width, items = plan.width, plan.items
    groups = plan.full // width
    low = jnp.bfloat16
    return pl.pallas_call(
        functools.partial(owner_kernel, plan, flip, rows),
        out_shape=jax.ShapeDtypeStruct((blocks_all, rows, columns), low),
        in_specs=[pl.BlockSpec(memory_space=pltpu.SMEM)] + [pl.BlockSpec(memory_space=pl.ANY)] * 2,
        out_specs=pl.BlockSpec(memory_space=pl.ANY),
        scratch_shapes=[
            pltpu.VMEM(pieces.shape, low),
            pltpu.VMEM(moments.shape, low),
            pltpu.VMEM((2, items, rows, columns), low),
            pltpu.VMEM((2, items, rows, columns), low),
            pltpu.VMEM((groups * width, rows, columns), low),
            pltpu.VMEM((groups, columns, columns), low),
            pltpu.VMEM((groups, columns, columns), low),
            pltpu.VMEM((columns, columns), jnp.float32),
            pltpu.VMEM((columns, columns), low),
            pltpu.VMEM((columns, columns), low),
            pltpu.SemaphoreType.DMA((2,)),
            pltpu.SemaphoreType.DMA((2, items)),
            pltpu.SemaphoreType.DMA((2, items)),
            pltpu.SemaphoreType.DMA((groups * width,)),
            pltpu.SemaphoreType.DMA((groups, width)),
            pltpu.SemaphoreType.DMA((groups, width)),
            pltpu.SemaphoreType.DMA((groups * width,)),
        ],
        compiler_params=pltpu.CompilerParams(
            collective_id=ident, has_side_effects=True, vmem_limit_bytes=50 * 1024 * 1024
        ),
        name=f"muon_owner_{ident}",
    )(table, pieces, moments)


def place_kernel(place, found, out_ref, held, wide, in_sem, out_sem):
    capacity = wide.shape[0]

    def bring(s):
        return pltpu.make_async_copy(found.at[place[0] + s], held.at[s], in_sem.at[s])

    def give(s):
        return pltpu.make_async_copy(wide.at[s], out_ref.at[0, s], out_sem.at[s])

    def start(s, carry):
        bring(s).start()
        return carry

    def widen(s, carry):
        bring(s).wait()
        piece = held[s].astype(jnp.float32)
        wide[s] = jnp.where(s < place[1], piece, jnp.zeros_like(piece))
        give(s).start()
        return carry

    def finish(s, carry):
        give(s).wait()
        return carry

    lax.fori_loop(0, capacity, start, 0, unroll=4)
    lax.fori_loop(0, capacity, widen, 0)
    lax.fori_loop(0, capacity, finish, 0, unroll=4)


def list_kernel(plans, capacity, owners, table, branch, place, order):
    n, last = len(plans), len(plans) - 1
    blocks_all, items = owners.shape[0], plans[0].items
    me = lax.axis_index("dp")

    def tally(b, held):
        return tuple(held[o] + (owners[b] == o).astype(jnp.int32) for o in range(n))

    held = lax.fori_loop(0, blocks_all, tally, (jnp.int32(0),) * n, unroll=8)
    fullest = jnp.int32(0)
    for o in range(n):
        fullest = jnp.where(held[o] == capacity, o, fullest)
    flip = fullest > last - fullest
    turn = jnp.minimum(fullest, last - fullest)
    ends = (held[0] >= plans[0].spare) & (held[last] >= plans[0].spare)
    base = []
    for o in range(n):
        total = jnp.int32(capacity)
        for other in range(n):
            if other != o:
                ahead = (flip == (other > o)) & (other != fullest)
                total = total + jnp.where(ahead, held[other], 0)
        base.append(jnp.where(fullest == o, 0, total))

    def put(b, free):
        owner = owners[b]
        where = free[n - 1]
        for o in range(n - 1):
            where = jnp.where(owner == o, free[o], where)
        order[where] = b
        return tuple(free[o] + (owner == o).astype(jnp.int32) for o in range(n))

    lax.fori_loop(0, blocks_all, put, tuple(base), unroll=8)
    begin, mine = base[n - 1], held[n - 1]
    for o in range(n - 1):
        begin, mine = jnp.where(me == o, base[o], begin), jnp.where(me == o, held[o], mine)
    at_last = jnp.where(flip, last - me, me) == last
    branch[0] = jnp.where(ends, fullest, n)
    place[0] = jnp.where(ends & (me != fullest), begin - capacity, 0)
    place[1] = mine

    known = [plan.positions() for plan in plans[: (n + 1) // 2]]
    for e in range(items):
        low, high = known[0][0][e], known[0][1][e]
        for k in range(1, len(known)):
            low, high = jnp.where(turn == k, known[k][0][e], low), jnp.where(turn == k, known[k][1][e], high)
        table[e] = order[low]
        table[items + e] = order[high]
        here = jnp.where(at_last, high, low) - begin
        table[2 * items + e] = jnp.clip(here, 0, capacity - 1)
        table[3 * items + e] = ((here >= 0) & (here < mine)).astype(jnp.int32)


def routed(gradients, momentum, owners):
    n, width = lax.axis_size("dp"), lax.axis_size("tensor")
    pieces, moments = gradients[0], momentum[0]
    blocks_all, rows, columns = pieces.shape
    capacity = moments.shape[0]
    last = n - 1
    plans = [Plan(n, width, blocks_all, capacity, width, min(p, last - p)) for p in range(n)]
    smem = pl.BlockSpec(memory_space=pltpu.SMEM)
    table, branch, place = pl.pallas_call(
        functools.partial(list_kernel, plans, capacity),
        out_shape=[jax.ShapeDtypeStruct((k,), jnp.int32) for k in (4 * plans[0].items, 1, 2)],
        in_specs=[smem],
        out_specs=[smem] * 3,
        scratch_shapes=[pltpu.SMEM((blocks_all,), jnp.int32)],
        name="muon_lists",
    )(owners)
    branches = [functools.partial(by_owner, plans[p], p > last - p, p + 1) for p in range(n)]
    branches.append(lambda table, g, m: fused(g, m, owners))
    found = lax.switch(branch[0], branches, table, pieces, moments)
    hbm = pl.BlockSpec(memory_space=pl.ANY)
    return pl.pallas_call(
        place_kernel,
        out_shape=jax.ShapeDtypeStruct((1, capacity, rows, columns), jnp.float32),
        in_specs=[smem, hbm],
        out_specs=hbm,
        scratch_shapes=[
            pltpu.VMEM((capacity, rows, columns), jnp.bfloat16),
            pltpu.VMEM((capacity, rows, columns), jnp.float32),
            pltpu.SemaphoreType.DMA((capacity,)),
            pltpu.SemaphoreType.DMA((capacity,)),
        ],
        compiler_params=pltpu.CompilerParams(vmem_limit_bytes=50 * 1024 * 1024),
        name="muon_place",
    )(place, found)


def choose(gradients, momentum, owners):
    n, width = lax.axis_size("dp"), lax.axis_size("tensor")
    blocks_all, rows = gradients.shape[1:3]
    capacity = momentum.shape[1]
    others = blocks_all - capacity
    even = blocks_all % (2 * width) == 0 and capacity % width == 0 and others % width == 0
    if n == 4 and even and width < others <= capacity and rows % 16 == 0 and others % (2 * width) == 0 and (blocks_all + 48) * capacity * blocks_all < 1 << 18 and width >= NS_TICKS:
        return routed(gradients, momentum, owners)
    return body(gradients, momentum, owners)


def solution(mesh):
    in_specs = (P("dp", None, "tensor", None), P("dp", None, "tensor", None), P())
    out_specs = P("dp", None, "tensor", None)
    return jax.shard_map(choose, mesh=mesh, in_specs=in_specs, out_specs=out_specs, check_vma=False)
```

```python
import functools
import math

import jax
import jax.numpy as jnp
from jax import lax
from jax.experimental import pallas as pl
from jax.experimental.pallas import tpu as pltpu
from jax.sharding import PartitionSpec as P

ITERS = 3


decay_rate = 0.95
newton_a = 3.4445
newton_b = -4.775
newton_c = 2.0315
norm_eps = 1e-07


def ranks_of(labels):
    length = labels.shape[0]
    places = jnp.arange(length, dtype=jnp.int32)
    earlier = (labels[None, :] == labels[:, None]) & (places[None, :] < places[:, None])
    return jnp.sum(earlier.astype(jnp.int32), axis=1)


def rows_at(array, index):
    count = array.shape[0]
    chosen = (index[:, None] == jnp.arange(count, dtype=jnp.int32)[None, :]).astype(array.dtype)
    picked = jnp.dot(chosen, array.reshape(count, -1), preferred_element_type=jnp.float32)
    return picked.astype(array.dtype).reshape((index.shape[0],) + array.shape[1:])


def dot(spec, left, right):
    return jnp.einsum(
        spec,
        left.astype(jnp.bfloat16),
        right.astype(jnp.bfloat16),
        preferred_element_type=jnp.float32,
    )


def iterate(blocks):
    widened = blocks.astype(jnp.float32) * (1.0 + decay_rate)
    lengths = jnp.sqrt(jnp.sum(widened * widened, axis=(1, 2), keepdims=True)) + norm_eps
    current = widened / lengths
    scale_up = math.sqrt(blocks.shape[1])
    for iteration in range(ITERS):
        squared = dot("kij,klj->kil", current, current)
        polynomial = newton_b * squared + newton_c * dot("kij,kjl->kil", squared, squared)
        current = newton_a * current + dot("kij,kjl->kil", polynomial, current)
    return current * scale_up


def body(gradients, momentum, owners):
    dp_count = lax.axis_size("dp")
    tp_count = lax.axis_size("tensor")
    my_group = lax.axis_index("dp")
    pieces = gradients[0]
    blocks_all, rows, columns = pieces.shape
    per_group = blocks_all // dp_count
    capacity = momentum.shape[1]
    slot_rank = ranks_of(owners)
    places = jnp.arange(blocks_all, dtype=jnp.int32)

    mine = owners == my_group
    moment = rows_at(momentum[0], jnp.minimum(slot_rank, capacity - 1))
    moment = jnp.where(mine[:, None, None], moment, jnp.zeros_like(moment)).astype(jnp.float32)
    ratio = decay_rate * decay_rate / (1.0 + decay_rate)
    folded = (pieces.astype(jnp.float32) + ratio * moment).astype(jnp.bfloat16)
    held = lax.psum_scatter(folded, "dp", scatter_dimension=0, tiled=True)

    per_device = (per_group + tp_count - 1) // tp_count
    padded_count = per_device * tp_count
    padded = jnp.pad(held, ((0, padded_count - per_group), (0, 0), (0, 0)))
    whole = lax.all_to_all(padded, "tensor", split_axis=0, concat_axis=1, tiled=True)
    finished = iterate(whole).astype(jnp.bfloat16)
    result = lax.all_to_all(finished, "tensor", split_axis=1, concat_axis=0, tiled=True)

    groups = jnp.arange(dp_count, dtype=jnp.int32)
    pair_most = (2 * per_group + dp_count - 1) // dp_count
    held_owner = lax.dynamic_slice_in_dim(owners, my_group * per_group, per_group)
    held_rank = ranks_of(held_owner)
    held_places = jnp.arange(per_group, dtype=jnp.int32)
    pair_ids = jnp.arange(pair_most, dtype=jnp.int32)
    matched = (held_owner[:, None, None] == groups[None, :, None]) & (
        held_rank[:, None, None] == pair_ids[None, None, :]
    )
    source = jnp.sum(jnp.where(matched, held_places[:, None, None], 0), axis=0).reshape(-1)
    outgoing = rows_at(result, source)
    outgoing = outgoing.reshape(dp_count, pair_most, rows, columns)
    incoming = lax.all_to_all(outgoing, "dp", split_axis=0, concat_axis=0, tiled=True)
    incoming = incoming.reshape(dp_count * pair_most, rows, columns)
    group_rank = ranks_of(owners * dp_count + places // per_group)
    position = places // per_group * pair_most + group_rank
    slot_ids = jnp.arange(capacity, dtype=jnp.int32)
    my_slots = mine[:, None] & (slot_rank[:, None] == slot_ids[None, :])
    occupied = jnp.any(my_slots, axis=0)
    arriving = jnp.sum(jnp.where(my_slots, position[:, None], 0), axis=0)
    chosen = rows_at(incoming, arriving).astype(jnp.float32)
    update = jnp.where(occupied[:, None, None], chosen, jnp.zeros_like(chosen))
    return update[None]


MESH = pl.DeviceIdType.MESH


def kernel(
    sizes, weight, slot, g_ref, m_ref, out_ref,
    arrived, partial, whole, ready, gathered, current,
    chain_send, chain_recv, scatter_send, scatter_recv, return_send, ahead_send, gather_recv, out_sem,
):
    n, width, half, rows, lead = sizes
    columns = g_ref.shape[2]
    z, t = lax.axis_index("dp"), lax.axis_index("tensor")
    per_device = half // width
    gap = half
    is_end = (z == 0) | (z == n - 1)
    low = 2 * z < n - 1

    barrier = pltpu.get_barrier_semaphore()

    @pl.when(z > 0)
    def _():
        pl.semaphore_signal(barrier, inc=1, device_id=(z - 1, t), device_id_type=MESH)

    @pl.when(z < n - 1)
    def _():
        pl.semaphore_signal(barrier, inc=1, device_id=(z + 1, t), device_id_type=MESH)

    def greet(k, carry):
        peer = lax.rem(t + k, width)
        pl.semaphore_signal(barrier, inc=1, device_id=(z, peer), device_id_type=MESH)
        return carry

    lax.fori_loop(1, width, greet, 0)
    pl.semaphore_wait(barrier, jnp.where(is_end, width, width + 1))

    def chain_copy(d, c):
        return pltpu.make_async_remote_copy(
            src_ref=partial.at[d, c],
            dst_ref=arrived.at[d, c],
            send_sem=chain_send.at[d, c],
            recv_sem=chain_recv.at[d, c],
            device_id=(z + 2 * d - 1, t),
            device_id_type=MESH,
        )

    def own(d, c):
        block = d * half + c
        moment = m_ref[slot[block]].astype(jnp.float32)
        return g_ref[block].astype(jnp.float32) + weight[block] * moment

    def my_rows(place):
        return pl.ds(pl.multiple_of(place * rows, rows), rows)

    def start_chain(d, c):
        partial[d, c] = own(d, c).astype(jnp.bfloat16)
        chain_copy(d, c).start()

    def add_chain(d, c):
        chain_copy(d, c).wait_recv()
        total = own(d, c) + arrived[d, c].astype(jnp.float32)
        partial[d, c] = total.astype(jnp.bfloat16)

    def scatter_copy(d, c, peer, sem):
        return pltpu.make_async_remote_copy(
            src_ref=partial.at[d, c],
            dst_ref=whole.at[c // width, my_rows(t)],
            send_sem=scatter_send.at[c],
            recv_sem=sem,
            device_id=(z, peer),
            device_id_type=MESH,
        )

    def return_copy(d, j, peer):
        block = d * half + j * width + t
        return pltpu.make_async_remote_copy(
            src_ref=ready.at[j, my_rows(peer)],
            dst_ref=gathered.at[block],
            send_sem=return_send.at[j, peer],
            recv_sem=gather_recv.at[block],
            device_id=(z, peer),
            device_id_type=MESH,
        )

    def ahead_copy(d, c):
        block = d * half + c
        return pltpu.make_async_remote_copy(
            src_ref=gathered.at[block],
            dst_ref=gathered.at[block],
            send_sem=ahead_send.at[block],
            recv_sem=gather_recv.at[block],
            device_id=(z + 1 - 2 * d, t),
            device_id_type=MESH,
        )

    def pass_on(d, c):
        ahead_copy(d, c).wait_recv()

        @pl.when((z + 1 - 2 * d >= 0) & (z + 1 - 2 * d < n))
        def _():
            ahead_copy(d, c).start()

    def iterate_in(j):
        widened = whole[j].astype(jnp.float32) * (1.0 + decay_rate)
        length = jnp.sqrt(jnp.sum(widened * widened)) + norm_eps
        current[...] = widened / length

        def once(k, carry):
            now = current[...]
            low_now = now.astype(jnp.bfloat16)
            squared = lax.dot_general(
                low_now, low_now, (((1,), (1,)), ((), ())), preferred_element_type=jnp.float32
            )
            low_squared = squared.astype(jnp.bfloat16)
            polynomial = newton_b * squared + newton_c * jnp.dot(
                low_squared, low_squared, preferred_element_type=jnp.float32
            )
            current[...] = newton_a * now + jnp.dot(
                polynomial.astype(jnp.bfloat16), low_now, preferred_element_type=jnp.float32
            )
            return carry

        lax.fori_loop(0, ITERS, once, 0)
        ready[j] = (current[...] * math.sqrt(columns)).astype(jnp.bfloat16)

    @pl.when(is_end)
    def _():
        near = jnp.where(z == 0, 0, 1)
        far = 1 - near

        def begin(c, carry):
            start_chain(far, c)
            return carry

        lax.fori_loop(0, half, begin, 0)

        def pass_group(j):
            def one(k, inner):
                pass_on(near, j * width + k)
                return inner

            lax.fori_loop(0, width, one, 0)

        def reduce_group(j):
            def chunk(k, inner):
                c = j * width + k
                add_chain(near, c)

                @pl.when(k == t)
                def _():
                    pltpu.make_async_copy(
                        partial.at[near, c], whole.at[j, my_rows(t)], scatter_recv.at[j, t]
                    ).start()

                @pl.when(k != t)
                def _():
                    scatter_copy(near, c, k, scatter_recv.at[j, t]).start()

                return inner

            lax.fori_loop(0, width, chunk, 0)

        def iterate_group(j):
            def land(k, inner):
                pltpu.make_async_copy(
                    partial.at[near, 0], whole.at[j, my_rows(k)], scatter_recv.at[j, k]
                ).wait()
                return inner

            lax.fori_loop(0, width, land, 0)
            iterate_in(j)

            def give(k, inner):
                @pl.when(k == t)
                def _():
                    block = near * half + j * width + t
                    pltpu.make_async_copy(
                        ready.at[j, my_rows(t)], gathered.at[block], gather_recv.at[block]
                    ).start()

                @pl.when(k != t)
                def _():
                    return_copy(near, j, k).start()

                return inner

            lax.fori_loop(0, width, give, 0)

        def block_step(j, carry):
            @pl.when(j < per_device)
            def _():
                reduce_group(j)

            @pl.when(j > 1)
            def _():
                pass_group(j - 2)

            @pl.when(j > 0)
            def _():
                iterate_group(j - 1)

            return carry

        lax.fori_loop(0, per_device + 1, block_step, 0)
        pass_group(per_device - 1)

        def finish(c, carry):
            pass_on(far, c)
            return carry

        lax.fori_loop(0, half, finish, 0)

    @pl.when(jnp.logical_not(is_end))
    def _():
        early = jnp.where(low, 1, 0)

        def forward(d, c):
            add_chain(d, c)
            chain_copy(d, c).start()

        def step(i, carry):
            @pl.when(i < half)
            def _():
                forward(early, i)

            @pl.when((i >= lead) & (i < half + lead))
            def _():
                forward(1 - early, i - lead)

            @pl.when((i >= gap) & (i < half + gap))
            def _():
                pass_on(1 - early, i - gap)

            @pl.when(i >= gap + lead)
            def _():
                pass_on(early, i - gap - lead)

            return carry

        lax.fori_loop(0, half + gap + lead, step, 0)

    final = pltpu.make_async_copy(gathered, out_ref, out_sem)
    final.start()

    for d in range(2):
        sink = 0 if d == 0 else n - 1

        def settle(c, carry):
            @pl.when(z != sink)
            def _():
                chain_copy(d, c).wait_send()

            @pl.when(z != n - 1 - sink)
            def _():
                ahead_copy(d, c).wait_send()

            @pl.when((z == sink) & (lax.rem(c, width) != t))
            def _():
                scatter_copy(d, c, lax.rem(c, width), scatter_recv.at[0, 0]).wait_send()
                return_copy(d, c // width, lax.rem(c, width)).wait_send()

            return carry

        lax.fori_loop(0, half, settle, 0)
    final.wait()


def pick_kernel(group, index, in_ref, out_ref):
    base = pl.program_id(0) * group
    for k in range(group):
        out_ref[k] = in_ref[index[base + k]]


def fused(pieces, moments, owners):
    n = lax.axis_size("dp")
    width = lax.axis_size("tensor")
    me = lax.axis_index("dp")
    blocks_all, rows, columns = pieces.shape
    capacity = moments.shape[0]
    half = blocks_all // 2
    lead = min(2, half)
    slot_rank = ranks_of(owners)
    mine = owners == me
    ratio = decay_rate * decay_rate / (1.0 + decay_rate)
    weight = jnp.where(mine, ratio, 0.0).astype(jnp.float32)
    slot = jnp.minimum(slot_rank, capacity - 1)
    order = columns
    low = jnp.bfloat16
    all_results = pl.pallas_call(
        functools.partial(kernel, (n, width, half, rows, lead)),
        out_shape=jax.ShapeDtypeStruct((blocks_all, rows, columns), low),
        in_specs=[
            pl.BlockSpec(memory_space=pltpu.SMEM),
            pl.BlockSpec(memory_space=pltpu.SMEM),
            pl.BlockSpec(memory_space=pltpu.VMEM),
            pl.BlockSpec(memory_space=pltpu.VMEM),
        ],
        out_specs=pl.BlockSpec(memory_space=pl.ANY),
        scratch_shapes=[
            pltpu.VMEM((2, half, rows, columns), low),
            pltpu.VMEM((2, half, rows, columns), low),
            pltpu.VMEM((half // width, order, columns), low),
            pltpu.VMEM((half // width, order, columns), low),
            pltpu.VMEM((blocks_all, rows, columns), low),
            pltpu.VMEM((order, columns), jnp.float32),
            pltpu.SemaphoreType.DMA((2, half)),
            pltpu.SemaphoreType.DMA((2, half)),
            pltpu.SemaphoreType.DMA((half,)),
            pltpu.SemaphoreType.DMA((half // width, width)),
            pltpu.SemaphoreType.DMA((half // width, width)),
            pltpu.SemaphoreType.DMA((blocks_all,)),
            pltpu.SemaphoreType.DMA((blocks_all,)),
            pltpu.SemaphoreType.DMA,
        ],
        compiler_params=pltpu.CompilerParams(
            collective_id=0, has_side_effects=True, vmem_limit_bytes=50 * 1024 * 1024
        ),
        name="muon_chain",
    )(weight, slot, pieces, moments)

    slot_ids = jnp.arange(capacity, dtype=jnp.int32)
    places = jnp.arange(blocks_all, dtype=jnp.int32)
    my_slots = mine[:, None] & (slot_rank[:, None] == slot_ids[None, :])
    index = jnp.sum(jnp.where(my_slots, places[:, None], 0), axis=0)
    index = jnp.pad(index, (0, blocks_all - capacity))
    group = math.gcd(blocks_all, 4)
    return pl.pallas_call(
        functools.partial(pick_kernel, group),
        out_shape=jax.ShapeDtypeStruct((blocks_all, rows, columns), low),
        grid_spec=pltpu.PrefetchScalarGridSpec(
            num_scalar_prefetch=1,
            grid=(blocks_all // group,),
            in_specs=[pl.BlockSpec(memory_space=pltpu.VMEM)],
            out_specs=pl.BlockSpec((group, rows, columns), lambda s, index: (s, 0, 0)),
        ),
        name="muon_pick",
    )(index, all_results)


AHEAD = 6
HOP = 4
SETTLE = 4
NS_TICKS = 2 * ITERS


def over(scaled, divisor):
    if isinstance(scaled, int):
        return scaled // divisor
    return (scaled * ((1 << 18) // divisor + 1)) >> 18


def at_most(limit, value):
    return min(limit, value) if isinstance(value, int) and isinstance(limit, int) else jnp.minimum(limit, value)


def pick(condition, yes, no):
    return (yes if condition else no) if isinstance(condition, bool) else jnp.where(condition, yes, no)


class Plan:
    def __init__(self, n, width, blocks_all, capacity, spare, place):
        self.n, self.width, self.place, self.last = n, width, place, n - 1
        self.full, self.spare = capacity, spare
        self.some = blocks_all - capacity - spare
        self.items = self.full + self.some
        self.batch = self.some // spare
        self.early = HOP - 1 if place == 0 else 0

    def firsts(self, e):
        if self.place == 0:
            span = self.items - self.early
            return at_most(self.full, over(e * self.full + span - 1, span))
        return over(e * self.full, self.items)

    def split(self, e):
        p = self.firsts(e)
        return self.firsts(e + 1) > p, p, e - p

    def item(self, first_kind, u):
        full, some, items, early = self.full, self.some, self.items, self.early
        if self.place == 0:
            span, rest = items - early, some - early
            first = over(u * span, full)
            other = at_most(over((u + 1) * span + rest - 1, rest) - 1, full + u)
        else:
            first = over((u + 1) * items + full - 1, full) - 1
            other = over(u * items, some)
        return jnp.where(first_kind, first, other)

    def shuffled(self, r):
        group = over(r, self.batch + 1)
        k = r - group * (self.batch + 1)
        return pick(k == self.batch, self.some + group, group * self.batch + k)

    def positions(self):
        low, high = [], []
        for e in range(self.items):
            is_first, p, q = self.split(e)
            low.append(p if is_first else self.full + q)
            if self.place == 0:
                high.append(self.full + min(self.shuffled(p), self.some + self.spare - 1))
            else:
                high.append(p if is_first else self.full + (self.some + q if q < self.spare else q))
        return low, high

    def targets(self, d, is_first):
        if self.place == 0:
            return jnp.where(is_first, 0, 1) if d == 0 else self.last
        return jnp.where(is_first, self.place, 0 if d == 0 else self.last)

    def carried(self, d, is_first):
        return is_first if self.place == 0 and d == 1 else True

    def works_on_firsts(self, f):
        return (f == 0) | (f == self.last) if self.place == 0 else f == self.place

    def skipped(self, f):
        if self.place == 0:
            return 0
        return jnp.where((f == 0) | (f == self.last) | (f == self.place), 0, self.spare)

    def landing(self, f, u):
        if self.place == 0:
            return jnp.where(f == self.last, self.shuffled(u), u)
        q = u + self.skipped(f)
        return jnp.where((f == self.last) & (q < self.spare), q + self.some, q)

    def other_item(self, e, q):
        if self.place == 0:
            return self.item(True, q + over(q, self.batch))
        return e


def owner_kernel(
    plan, flip, rows, table, g_hbm, m_hbm, out_ref,
    g_ref, m_ref, arrived, partial, total, whole, ready, current, low_current, low_poly,
    load_sem, chain_send, chain_recv, scatter_send, scatter_recv, return_send, gather_recv,
):
    n, width, items = plan.n, plan.width, plan.items
    columns = g_ref.shape[2]
    z, t = lax.axis_index("dp"), lax.axis_index("tensor")
    f = n - 1 - z if flip else z
    step = (1, -1) if flip else (-1, 1)
    groups_most = whole.shape[0]
    low = jnp.bfloat16

    load_g = pltpu.make_async_copy(g_hbm, g_ref, load_sem.at[0])
    load_m = pltpu.make_async_copy(m_hbm, m_ref, load_sem.at[1])
    load_g.start()
    load_m.start()

    barrier = pltpu.get_barrier_semaphore()

    @pl.when(z > 0)
    def _():
        pl.semaphore_signal(barrier, inc=1, device_id=(z - 1, t), device_id_type=MESH)

    @pl.when(z < n - 1)
    def _():
        pl.semaphore_signal(barrier, inc=1, device_id=(z + 1, t), device_id_type=MESH)

    def greet(k, carry):
        peer = lax.rem(t + k, width)
        pl.semaphore_signal(barrier, inc=1, device_id=(z, peer), device_id_type=MESH)
        return carry

    lax.fori_loop(1, width, greet, 0)
    pl.semaphore_wait(barrier, jnp.where((z == 0) | (z == n - 1), width, width + 1))
    load_g.wait()
    load_m.wait()

    on_firsts = plan.works_on_firsts(f)
    skipped = plan.skipped(f)
    count = jnp.where(on_firsts, plan.full, plan.some - skipped)
    groups = count // width
    lag_low = HOP * (n - 1 - f)
    lag_high = HOP * f
    lag = jnp.where(f == 0, lag_low, jnp.where(f == n - 1, lag_high, jnp.maximum(lag_low, lag_high)))

    def my_rows(place):
        return pl.ds(pl.multiple_of(place * rows, rows), rows)

    spread = width // 2
    my_turn = t // 2 + lax.rem(t, 2) * spread

    def peer_of(u):
        k = lax.rem(u, width)
        return lax.rem(k, spread) * 2 + k // spread

    def chain_copy(d, e):
        return pltpu.make_async_remote_copy(
            src_ref=partial.at[d, e],
            dst_ref=arrived.at[d, e],
            send_sem=chain_send.at[d],
            recv_sem=chain_recv.at[d, e],
            device_id=(z + step[d], t),
            device_id_type=MESH,
        )

    def scatter_copy(u, peer):
        j = u // width
        return pltpu.make_async_remote_copy(
            src_ref=total.at[u],
            dst_ref=whole.at[j, my_rows(t)],
            send_sem=scatter_send,
            recv_sem=scatter_recv.at[j],
            device_id=(z, peer),
            device_id_type=MESH,
        )

    def return_copy(u, peer):
        j = u // width
        return pltpu.make_async_remote_copy(
            src_ref=ready.at[j, my_rows(peer)],
            dst_ref=out_ref.at[plan.landing(f, u)],
            send_sem=return_send,
            recv_sem=gather_recv,
            device_id=(z, peer),
            device_id_type=MESH,
        )

    def takes_part(d, e):
        is_first = plan.split(e)[0]
        target = plan.targets(d, is_first)
        inside = (e >= 0) & (e < items) & plan.carried(d, is_first)
        if d == 0:
            return inside & (f >= target) & (f < n - 1), inside & (f > target)
        return inside & (f <= target) & (f > 0), inside & (f < target)

    def flow(d, e):
        receives, sends = takes_part(d, e)
        blocks = d * items + e

        @pl.when(receives)
        def _():
            chain_copy(d, e).wait_recv()

        @pl.when(sends & receives)
        def _():
            mixed = g_ref[table[blocks]].astype(jnp.float32) + arrived[d, e].astype(jnp.float32)
            partial[d, e] = mixed.astype(low)

        @pl.when(sends & jnp.logical_not(receives))
        def _():
            partial[d, e] = g_ref[table[blocks]]

        @pl.when(sends)
        def _():
            chain_copy(d, e).start()

    def candidate(e, u):
        def own(d):
            weight = table[3 * items + e].astype(jnp.float32) * (decay_rate * decay_rate / (1.0 + decay_rate))
            moment = m_ref[table[2 * items + e]].astype(jnp.float32)
            return g_ref[table[d * items + e]].astype(jnp.float32) + weight * moment

        @pl.when(f == 0)
        def _():
            total[u] = (own(0) + arrived[0, e].astype(jnp.float32)).astype(low)

        @pl.when(f == n - 1)
        def _():
            total[u] = (own(1) + arrived[1, e].astype(jnp.float32)).astype(low)

        @pl.when((f > 0) & (f < n - 1))
        def _():
            twin = plan.other_item(e, u + skipped)
            both = arrived[0, e].astype(jnp.float32) + arrived[1, twin].astype(jnp.float32)
            total[u] = (own(0) + both).astype(low)

        peer = peer_of(u)

        @pl.when(peer == t)
        def _():
            whole[u // width, my_rows(t)] = total[u]

        @pl.when(peer != t)
        def _():
            scatter_copy(u, peer).start()

    def begin_block(j):
        most = pl.ds(0, (width - 1) * rows)
        pltpu.make_async_copy(ready.at[j, most], whole.at[j, most], scatter_recv.at[j]).wait()
        widened = whole[j].astype(jnp.float32) * (1.0 + decay_rate)
        length = jnp.sqrt(jnp.sum(widened * widened)) + norm_eps
        start = widened / length
        current[...] = start
        low_current[...] = start.astype(low)

    def make_polynomial():
        now = low_current[...]
        squared = lax.dot_general(now, now, (((1,), (1,)), ((), ())), preferred_element_type=jnp.float32)
        low_squared = squared.astype(low)
        polynomial = newton_b * squared + newton_c * jnp.dot(
            low_squared, low_squared, preferred_element_type=jnp.float32
        )
        low_poly[...] = polynomial.astype(low)

    def apply_polynomial():
        later = newton_a * current[...] + jnp.dot(
            low_poly[...], low_current[...], preferred_element_type=jnp.float32
        )
        current[...] = later
        low_current[...] = later.astype(low)

    def finish_block(j):
        ready[j] = (current[...] * math.sqrt(columns)).astype(low)
        u = j * width + my_turn

        def give(k, carry):
            return_copy(u, lax.rem(t + k, width)).start()
            return carry

        pltpu.make_async_copy(
            ready.at[j, my_rows(t)], out_ref.at[plan.landing(f, u)], gather_recv
        ).start()
        lax.fori_loop(1, width, give, 0)

    def tick(moment, carry):
        i = moment - AHEAD
        flow(0, i - lag_low + jnp.where(f == n - 1, AHEAD, 0))
        flow(1, i - lag_high + jnp.where(f == 0, AHEAD, 0))
        e = i - lag
        is_first, p, q = plan.split(e)
        u = jnp.where(on_firsts, p, q - skipped)

        @pl.when((is_first == on_firsts) & (e >= 0) & (e < items) & (u >= 0))
        def _():
            candidate(e, u)

        since = jnp.maximum(e - SETTLE, -1)
        firsts = plan.firsts(since + 1)
        known = jnp.minimum(jnp.where(on_firsts, firsts, since + 1 - firsts - skipped), count)
        j = jnp.maximum(known - 1 - my_turn, 0) // width
        phase = since - plan.item(on_firsts, j * width + my_turn + jnp.where(on_firsts, 0, skipped))
        active = (known > my_turn) & (phase < NS_TICKS)

        @pl.when(active & (phase == 0))
        def _():
            begin_block(j)

        @pl.when(active & (phase % 2 == 0))
        def _():
            make_polynomial()

        @pl.when(active & (phase % 2 == 1))
        def _():
            apply_polynomial()

        @pl.when(active & (phase == NS_TICKS - 1))
        def _():
            finish_block(j)

        return carry

    lax.fori_loop(0, AHEAD + items + HOP * (n - 1) + SETTLE + NS_TICKS, tick, 0)

    def drain(held, amount, sem):
        part = held.at[pl.ds(0, amount)]
        pltpu.make_async_copy(part, part, sem).wait()

    for d in range(2):
        sends = []
        for is_first in (True, False):
            target = plan.targets(d, is_first)
            sends.append(plan.carried(d, is_first) & (f > target if d == 0 else f < target))

        for kinds, amount in (((True, True), plan.items), ((True, False), plan.full), ((False, True), plan.some)):

            @pl.when((sends[0] == kinds[0]) & (sends[1] == kinds[1]))
            def _():
                drain(partial.at[d], amount, chain_send.at[d])

    for most in range(1, groups_most + 1):

        @pl.when(groups == most)
        def _():
            drain(total, most * (width - 1), scatter_send)
            drain(total, most * (width - 1), return_send)
            drain(total, most * width, gather_recv)


def by_owner(plan, flip, ident, table, pieces, moments):
    blocks_all, rows, columns = pieces.shape
    width, items = plan.width, plan.items
    groups = plan.full // width
    low = jnp.bfloat16
    return pl.pallas_call(
        functools.partial(owner_kernel, plan, flip, rows),
        out_shape=jax.ShapeDtypeStruct((blocks_all, rows, columns), low),
        in_specs=[pl.BlockSpec(memory_space=pltpu.SMEM)] + [pl.BlockSpec(memory_space=pl.ANY)] * 2,
        out_specs=pl.BlockSpec(memory_space=pl.ANY),
        scratch_shapes=[
            pltpu.VMEM(pieces.shape, low),
            pltpu.VMEM(moments.shape, low),
            pltpu.VMEM((2, items, rows, columns), low),
            pltpu.VMEM((2, items, rows, columns), low),
            pltpu.VMEM((groups * width, rows, columns), low),
            pltpu.VMEM((groups, columns, columns), low),
            pltpu.VMEM((groups, columns, columns), low),
            pltpu.VMEM((columns, columns), jnp.float32),
            pltpu.VMEM((columns, columns), low),
            pltpu.VMEM((columns, columns), low),
            pltpu.SemaphoreType.DMA((2,)),
            pltpu.SemaphoreType.DMA((2,)),
            pltpu.SemaphoreType.DMA((2, items)),
            pltpu.SemaphoreType.DMA,
            pltpu.SemaphoreType.DMA((groups,)),
            pltpu.SemaphoreType.DMA,
            pltpu.SemaphoreType.DMA,
        ],
        compiler_params=pltpu.CompilerParams(
            collective_id=ident, has_side_effects=True, vmem_limit_bytes=50 * 1024 * 1024
        ),
        name=f"muon_owner_{ident}",
    )(table, pieces, moments)


def place_kernel(place, found, out_ref, held, wide, in_sem, out_sem):
    capacity = wide.shape[0]

    def bring(s):
        return pltpu.make_async_copy(found.at[place[0] + s], held.at[s], in_sem.at[s])

    def give(s):
        return pltpu.make_async_copy(wide.at[s], out_ref.at[0, s], out_sem.at[s])

    def start(s, carry):
        bring(s).start()
        return carry

    def widen(s, carry):
        bring(s).wait()
        piece = held[s].astype(jnp.float32)
        wide[s] = jnp.where(s < place[1], piece, jnp.zeros_like(piece))
        give(s).start()
        return carry

    def finish(s, carry):
        give(s).wait()
        return carry

    lax.fori_loop(0, capacity, start, 0, unroll=4)
    lax.fori_loop(0, capacity, widen, 0)
    lax.fori_loop(0, capacity, finish, 0, unroll=4)


def list_kernel(plans, capacity, owners, table, branch, place, order):
    n, last = len(plans), len(plans) - 1
    blocks_all, items = owners.shape[0], plans[0].items
    me = lax.axis_index("dp")

    def tally(b, held):
        return tuple(held[o] + (owners[b] == o).astype(jnp.int32) for o in range(n))

    held = lax.fori_loop(0, blocks_all, tally, (jnp.int32(0),) * n, unroll=8)
    fullest = jnp.int32(0)
    for o in range(n):
        fullest = jnp.where(held[o] == capacity, o, fullest)
    flip = fullest > last - fullest
    turn = jnp.minimum(fullest, last - fullest)
    ends = (held[0] >= plans[0].spare) & (held[last] >= plans[0].spare)
    base = []
    for o in range(n):
        total = jnp.int32(capacity)
        for other in range(n):
            if other != o:
                ahead = (flip == (other > o)) & (other != fullest)
                total = total + jnp.where(ahead, held[other], 0)
        base.append(jnp.where(fullest == o, 0, total))

    def put(b, free):
        owner = owners[b]
        where = free[n - 1]
        for o in range(n - 1):
            where = jnp.where(owner == o, free[o], where)
        order[where] = b
        return tuple(free[o] + (owner == o).astype(jnp.int32) for o in range(n))

    lax.fori_loop(0, blocks_all, put, tuple(base), unroll=8)
    begin, mine = base[n - 1], held[n - 1]
    for o in range(n - 1):
        begin, mine = jnp.where(me == o, base[o], begin), jnp.where(me == o, held[o], mine)
    at_last = jnp.where(flip, last - me, me) == last
    branch[0] = jnp.where(ends, fullest, n)
    place[0] = jnp.where(ends & (me != fullest), begin - capacity, 0)
    place[1] = mine

    known = [plan.positions() for plan in plans[: (n + 1) // 2]]
    for e in range(items):
        low, high = known[0][0][e], known[0][1][e]
        for k in range(1, len(known)):
            low, high = jnp.where(turn == k, known[k][0][e], low), jnp.where(turn == k, known[k][1][e], high)
        table[e] = order[low]
        table[items + e] = order[high]
        here = jnp.where(at_last, high, low) - begin
        table[2 * items + e] = jnp.clip(here, 0, capacity - 1)
        table[3 * items + e] = ((here >= 0) & (here < mine)).astype(jnp.int32)


def routed(gradients, momentum, owners):
    n, width = lax.axis_size("dp"), lax.axis_size("tensor")
    pieces, moments = gradients[0], momentum[0]
    blocks_all, rows, columns = pieces.shape
    capacity = moments.shape[0]
    last = n - 1
    plans = [Plan(n, width, blocks_all, capacity, width, min(p, last - p)) for p in range(n)]
    smem = pl.BlockSpec(memory_space=pltpu.SMEM)
    table, branch, place = pl.pallas_call(
        functools.partial(list_kernel, plans, capacity),
        out_shape=[jax.ShapeDtypeStruct((k,), jnp.int32) for k in (4 * plans[0].items, 1, 2)],
        in_specs=[smem],
        out_specs=[smem] * 3,
        scratch_shapes=[pltpu.SMEM((blocks_all,), jnp.int32)],
        name="muon_lists",
    )(owners)
    branches = [functools.partial(by_owner, plans[p], p > last - p, p + 1) for p in range(n)]
    branches.append(lambda table, g, m: fused(g, m, owners))
    found = lax.switch(branch[0], branches, table, pieces, moments)
    hbm = pl.BlockSpec(memory_space=pl.ANY)
    return pl.pallas_call(
        place_kernel,
        out_shape=jax.ShapeDtypeStruct((1, capacity, rows, columns), jnp.float32),
        in_specs=[smem, hbm],
        out_specs=hbm,
        scratch_shapes=[
            pltpu.VMEM((capacity, rows, columns), jnp.bfloat16),
            pltpu.VMEM((capacity, rows, columns), jnp.float32),
            pltpu.SemaphoreType.DMA((capacity,)),
            pltpu.SemaphoreType.DMA((capacity,)),
        ],
        compiler_params=pltpu.CompilerParams(vmem_limit_bytes=50 * 1024 * 1024),
        name="muon_place",
    )(place, found)


def choose(gradients, momentum, owners):
    n, width = lax.axis_size("dp"), lax.axis_size("tensor")
    blocks_all, rows = gradients.shape[1:3]
    capacity = momentum.shape[1]
    others = blocks_all - capacity
    even = blocks_all % (2 * width) == 0 and capacity % width == 0 and others % width == 0
    if n == 4 and even and width < others <= capacity and rows % 16 == 0 and others % (2 * width) == 0 and (blocks_all + 48) * capacity * blocks_all < 1 << 18 and width >= NS_TICKS:
        return routed(gradients, momentum, owners)
    return body(gradients, momentum, owners)


def solution(mesh):
    in_specs = (P("dp", None, "tensor", None), P("dp", None, "tensor", None), P())
    out_specs = P("dp", None, "tensor", None)
    return jax.shard_map(choose, mesh=mesh, in_specs=in_specs, out_specs=out_specs, check_vma=False)
```

```python
import functools
import math

import jax
import jax.numpy as jnp
from jax import lax
from jax.experimental import pallas as pl
from jax.experimental.pallas import tpu as pltpu
from jax.sharding import PartitionSpec as P

ITERS = 3


decay_rate = 0.95
newton_a = 3.4445
newton_b = -4.775
newton_c = 2.0315
norm_eps = 1e-07


def ranks_of(labels):
    length = labels.shape[0]
    places = jnp.arange(length, dtype=jnp.int32)
    earlier = (labels[None, :] == labels[:, None]) & (places[None, :] < places[:, None])
    return jnp.sum(earlier.astype(jnp.int32), axis=1)


def rows_at(array, index):
    count = array.shape[0]
    chosen = (index[:, None] == jnp.arange(count, dtype=jnp.int32)[None, :]).astype(array.dtype)
    picked = jnp.dot(chosen, array.reshape(count, -1), preferred_element_type=jnp.float32)
    return picked.astype(array.dtype).reshape((index.shape[0],) + array.shape[1:])


def dot(spec, left, right):
    return jnp.einsum(
        spec,
        left.astype(jnp.bfloat16),
        right.astype(jnp.bfloat16),
        preferred_element_type=jnp.float32,
    )


def iterate(blocks):
    widened = blocks.astype(jnp.float32) * (1.0 + decay_rate)
    lengths = jnp.sqrt(jnp.sum(widened * widened, axis=(1, 2), keepdims=True)) + norm_eps
    current = widened / lengths
    scale_up = math.sqrt(blocks.shape[1])
    for iteration in range(ITERS):
        squared = dot("kij,klj->kil", current, current)
        polynomial = newton_b * squared + newton_c * dot("kij,kjl->kil", squared, squared)
        current = newton_a * current + dot("kij,kjl->kil", polynomial, current)
    return current * scale_up


def body(gradients, momentum, owners):
    dp_count = lax.axis_size("dp")
    tp_count = lax.axis_size("tensor")
    my_group = lax.axis_index("dp")
    pieces = gradients[0]
    blocks_all, rows, columns = pieces.shape
    per_group = blocks_all // dp_count
    capacity = momentum.shape[1]
    slot_rank = ranks_of(owners)
    places = jnp.arange(blocks_all, dtype=jnp.int32)

    mine = owners == my_group
    moment = rows_at(momentum[0], jnp.minimum(slot_rank, capacity - 1))
    moment = jnp.where(mine[:, None, None], moment, jnp.zeros_like(moment)).astype(jnp.float32)
    ratio = decay_rate * decay_rate / (1.0 + decay_rate)
    folded = (pieces.astype(jnp.float32) + ratio * moment).astype(jnp.bfloat16)
    held = lax.psum_scatter(folded, "dp", scatter_dimension=0, tiled=True)

    per_device = (per_group + tp_count - 1) // tp_count
    padded_count = per_device * tp_count
    padded = jnp.pad(held, ((0, padded_count - per_group), (0, 0), (0, 0)))
    whole = lax.all_to_all(padded, "tensor", split_axis=0, concat_axis=1, tiled=True)
    finished = iterate(whole).astype(jnp.bfloat16)
    result = lax.all_to_all(finished, "tensor", split_axis=1, concat_axis=0, tiled=True)

    groups = jnp.arange(dp_count, dtype=jnp.int32)
    pair_most = (2 * per_group + dp_count - 1) // dp_count
    held_owner = lax.dynamic_slice_in_dim(owners, my_group * per_group, per_group)
    held_rank = ranks_of(held_owner)
    held_places = jnp.arange(per_group, dtype=jnp.int32)
    pair_ids = jnp.arange(pair_most, dtype=jnp.int32)
    matched = (held_owner[:, None, None] == groups[None, :, None]) & (
        held_rank[:, None, None] == pair_ids[None, None, :]
    )
    source = jnp.sum(jnp.where(matched, held_places[:, None, None], 0), axis=0).reshape(-1)
    outgoing = rows_at(result, source)
    outgoing = outgoing.reshape(dp_count, pair_most, rows, columns)
    incoming = lax.all_to_all(outgoing, "dp", split_axis=0, concat_axis=0, tiled=True)
    incoming = incoming.reshape(dp_count * pair_most, rows, columns)
    group_rank = ranks_of(owners * dp_count + places // per_group)
    position = places // per_group * pair_most + group_rank
    slot_ids = jnp.arange(capacity, dtype=jnp.int32)
    my_slots = mine[:, None] & (slot_rank[:, None] == slot_ids[None, :])
    occupied = jnp.any(my_slots, axis=0)
    arriving = jnp.sum(jnp.where(my_slots, position[:, None], 0), axis=0)
    chosen = rows_at(incoming, arriving).astype(jnp.float32)
    update = jnp.where(occupied[:, None, None], chosen, jnp.zeros_like(chosen))
    return update[None]


MESH = pl.DeviceIdType.MESH


AHEAD = 6
HOP = 4
SETTLE = 6
NS_TICKS = 2 * ITERS


def over(scaled, divisor):
    if isinstance(scaled, int):
        return scaled // divisor
    return (scaled * ((1 << 18) // divisor + 1)) >> 18


def at_most(limit, value):
    return min(limit, value) if isinstance(value, int) and isinstance(limit, int) else jnp.minimum(limit, value)


def pick(condition, yes, no):
    return (yes if condition else no) if isinstance(condition, bool) else jnp.where(condition, yes, no)


class Plan:
    def __init__(self, n, width, blocks_all, capacity, spare, place):
        self.n, self.width, self.place, self.last = n, width, place, n - 1
        self.full, self.spare = capacity, spare
        self.some = blocks_all - capacity - spare
        self.items = self.full + self.some
        self.batch = self.some // spare if spare else self.some
        self.early = HOP - 1 if place == 0 else 0

    def firsts(self, e):
        if self.place == 0:
            span = self.items - self.early
            return at_most(self.full, over(e * self.full + span - 1, span))
        return over(e * self.full, self.items)

    def split(self, e):
        p = self.firsts(e)
        return self.firsts(e + 1) > p, p, e - p

    def item(self, first_kind, u):
        full, some, items, early = self.full, self.some, self.items, self.early
        if self.place == 0:
            span, rest = items - early, some - early
            first = over(u * span, full)
            other = at_most(over((u + 1) * span + rest - 1, rest) - 1, full + u)
        else:
            first = over((u + 1) * items + full - 1, full) - 1
            other = over(u * items, some)
        return jnp.where(first_kind, first, other)

    def shuffled(self, r):
        group = over(r, self.batch + 1)
        k = r - group * (self.batch + 1)
        return pick(k == self.batch, self.some + group, group * self.batch + k)

    def positions(self):
        low, high = [], []
        for e in range(self.items):
            is_first, p, q = self.split(e)
            low.append(p if is_first else self.full + q)
            if self.place == 0:
                high.append(self.full + min(self.shuffled(p), self.some + self.spare - 1))
            else:
                high.append(p if is_first else self.full + (self.some + q if q < self.spare else q))
        return low, high

    def targets(self, d, is_first):
        if self.place == 0:
            return jnp.where(is_first, 0, 1) if d == 0 else self.last
        return jnp.where(is_first, self.place, 0 if d == 0 else self.last)

    def carried(self, d, is_first):
        return is_first if self.place == 0 and d == 1 else True

    def works_on_firsts(self, f):
        return (f == 0) | (f == self.last) if self.place == 0 else f == self.place

    def skipped(self, f):
        if self.place == 0:
            return 0
        return jnp.where((f == 0) | (f == self.last) | (f == self.place), 0, self.spare)

    def landing(self, f, u):
        if self.place == 0:
            return jnp.where(f == self.last, self.shuffled(u), u)
        q = u + self.skipped(f)
        return jnp.where((f == self.last) & (q < self.spare), q + self.some, q)

    def other_item(self, e, q):
        if self.place == 0:
            return self.item(True, q + over(q, self.batch))
        return e


def owner_kernel(
    plan, flip, rows, table, g_hbm, m_hbm, out_ref,
    g_ref, m_ref, arrived, partial, total, whole, ready, current, low_current, low_poly,
    load_sem, chain_send, chain_recv, scatter_send, scatter_recv, return_send, gather_recv,
):
    n, width, items = plan.n, plan.width, plan.items
    stride = g_ref.shape[0]
    columns = g_ref.shape[2]
    z, t = lax.axis_index("dp"), lax.axis_index("tensor")
    f = n - 1 - z if flip else z
    step = (1, -1) if flip else (-1, 1)
    groups_most = whole.shape[0]
    low = jnp.bfloat16

    load_g = pltpu.make_async_copy(g_hbm, g_ref, load_sem.at[0])
    load_m = pltpu.make_async_copy(m_hbm, m_ref, load_sem.at[1])
    load_g.start()
    load_m.start()

    barrier = pltpu.get_barrier_semaphore()

    @pl.when(z > 0)
    def _():
        pl.semaphore_signal(barrier, inc=1, device_id=(z - 1, t), device_id_type=MESH)

    @pl.when(z < n - 1)
    def _():
        pl.semaphore_signal(barrier, inc=1, device_id=(z + 1, t), device_id_type=MESH)

    def greet(k, carry):
        peer = lax.rem(t + k, width)
        pl.semaphore_signal(barrier, inc=1, device_id=(z, peer), device_id_type=MESH)
        return carry

    lax.fori_loop(1, width, greet, 0)
    pl.semaphore_wait(barrier, jnp.where((z == 0) | (z == n - 1), width, width + 1))
    load_g.wait()

    on_firsts = plan.works_on_firsts(f)
    skipped = plan.skipped(f)
    count = jnp.where(on_firsts, plan.full, plan.some - skipped)
    groups = count // width
    lag_low = HOP * (n - 1 - f)
    lag_high = HOP * f
    lag = jnp.where(f == 0, lag_low, jnp.where(f == n - 1, lag_high, jnp.maximum(lag_low, lag_high)))

    def my_rows(place):
        return pl.ds(pl.multiple_of(place * rows, rows), rows)

    spread = width // 2
    my_turn = t // 2 + lax.rem(t, 2) * spread

    def peer_of(u):
        k = lax.rem(u, width)
        return lax.rem(k, spread) * 2 + k // spread

    def chain_copy(d, e):
        return pltpu.make_async_remote_copy(
            src_ref=partial.at[d, e],
            dst_ref=arrived.at[d, e],
            send_sem=chain_send.at[d],
            recv_sem=chain_recv.at[d, e],
            device_id=(z + step[d], t),
            device_id_type=MESH,
        )

    def scatter_copy(u, peer):
        j = u // width
        return pltpu.make_async_remote_copy(
            src_ref=total.at[u],
            dst_ref=whole.at[j, my_rows(t)],
            send_sem=scatter_send,
            recv_sem=scatter_recv.at[j],
            device_id=(z, peer),
            device_id_type=MESH,
        )

    def return_copy(u, peer):
        j = u // width
        return pltpu.make_async_remote_copy(
            src_ref=ready.at[j, my_rows(peer)],
            dst_ref=out_ref.at[plan.landing(f, u)],
            send_sem=return_send,
            recv_sem=gather_recv,
            device_id=(z, peer),
            device_id_type=MESH,
        )

    def takes_part(d, e):
        is_first = plan.split(e)[0]
        target = plan.targets(d, is_first)
        inside = (e >= 0) & (e < items) & plan.carried(d, is_first)
        if d == 0:
            return inside & (f >= target) & (f < n - 1), inside & (f > target)
        return inside & (f <= target) & (f > 0), inside & (f < target)

    def flow(d, e):
        receives, sends = takes_part(d, e)
        blocks = d * stride + e

        @pl.when(receives)
        def _():
            chain_copy(d, e).wait_recv()

        @pl.when(sends & receives)
        def _():
            mixed = g_ref[table[blocks]].astype(jnp.float32) + arrived[d, e].astype(jnp.float32)
            partial[d, e] = mixed.astype(low)

        @pl.when(sends & jnp.logical_not(receives))
        def _():
            partial[d, e] = g_ref[table[blocks]]

        @pl.when(sends)
        def _():
            chain_copy(d, e).start()

    def candidate(e, u):
        def own(d):
            weight = table[3 * stride + e].astype(jnp.float32) * (decay_rate * decay_rate / (1.0 + decay_rate))
            moment = m_ref[table[2 * stride + e]].astype(jnp.float32)
            return g_ref[table[d * stride + e]].astype(jnp.float32) + weight * moment

        @pl.when(f == 0)
        def _():
            total[u] = (own(0) + arrived[0, e].astype(jnp.float32)).astype(low)

        @pl.when(f == n - 1)
        def _():
            total[u] = (own(1) + arrived[1, e].astype(jnp.float32)).astype(low)

        @pl.when((f > 0) & (f < n - 1))
        def _():
            twin = plan.other_item(e, u + skipped)
            both = arrived[0, e].astype(jnp.float32) + arrived[1, twin].astype(jnp.float32)
            total[u] = (own(0) + both).astype(low)

        peer = peer_of(u)

        @pl.when(peer == t)
        def _():
            whole[u // width, my_rows(t)] = total[u]

        @pl.when(peer != t)
        def _():
            scatter_copy(u, peer).start()

    def begin_block(j):
        most = pl.ds(0, (width - 1) * rows)
        pltpu.make_async_copy(ready.at[j, most], whole.at[j, most], scatter_recv.at[j]).wait()
        widened = whole[j].astype(jnp.float32) * (1.0 + decay_rate)
        length = jnp.sqrt(jnp.sum(widened * widened)) + norm_eps
        start = widened / length
        current[...] = start
        low_current[...] = start.astype(low)

    def make_polynomial():
        now = low_current[...]
        squared = lax.dot_general(now, now, (((1,), (1,)), ((), ())), preferred_element_type=jnp.float32)
        low_squared = squared.astype(low)
        polynomial = newton_b * squared + newton_c * jnp.dot(
            low_squared, low_squared, preferred_element_type=jnp.float32
        )
        low_poly[...] = polynomial.astype(low)

    def apply_polynomial():
        later = newton_a * current[...] + jnp.dot(
            low_poly[...], low_current[...], preferred_element_type=jnp.float32
        )
        current[...] = later
        low_current[...] = later.astype(low)

    def finish_block(j):
        ready[j] = (current[...] * math.sqrt(columns)).astype(low)
        u = j * width + my_turn

        def give(k, carry):
            return_copy(u, lax.rem(t + k, width)).start()
            return carry

        pltpu.make_async_copy(
            ready.at[j, my_rows(t)], out_ref.at[plan.landing(f, u)], gather_recv
        ).start()
        lax.fori_loop(1, width, give, 0)

    def tick(moment, carry):
        i = moment - AHEAD

        @pl.when(i == 0)
        def _():
            load_m.wait()

        flow(0, i - lag_low + jnp.where(f == n - 1, AHEAD, 0))
        flow(1, i - lag_high + jnp.where(f == 0, AHEAD, 0))
        e = i - lag
        is_first, p, q = plan.split(e)
        u = jnp.where(on_firsts, p, q - skipped)

        @pl.when((is_first == on_firsts) & (e >= 0) & (e < items) & (u >= 0))
        def _():
            candidate(e, u)

        since = jnp.maximum(e - SETTLE, -1)
        firsts = plan.firsts(since + 1)
        known = jnp.minimum(jnp.where(on_firsts, firsts, since + 1 - firsts - skipped), count)
        j = jnp.maximum(known - 1 - my_turn, 0) // width
        phase = since - plan.item(on_firsts, j * width + my_turn + jnp.where(on_firsts, 0, skipped))
        active = (known > my_turn) & (phase < NS_TICKS)

        @pl.when(active & (phase == 0))
        def _():
            begin_block(j)

        @pl.when(active & (phase % 2 == 0))
        def _():
            make_polynomial()

        @pl.when(active & (phase % 2 == 1))
        def _():
            apply_polynomial()

        @pl.when(active & (phase == NS_TICKS - 1))
        def _():
            finish_block(j)

        return carry

    lax.fori_loop(0, AHEAD + items + HOP * (n - 1) + SETTLE + NS_TICKS, tick, 0)

    def drain(held, amount, sem):
        part = held.at[pl.ds(0, amount)]
        pltpu.make_async_copy(part, part, sem).wait()

    for d in range(2):
        sends = []
        for is_first in (True, False):
            target = plan.targets(d, is_first)
            sends.append(plan.carried(d, is_first) & (f > target if d == 0 else f < target))

        for kinds, amount in (((True, True), plan.items), ((True, False), plan.full), ((False, True), plan.some)):

            @pl.when((sends[0] == kinds[0]) & (sends[1] == kinds[1]))
            def _():
                drain(partial.at[d], amount, chain_send.at[d])

    for most in range(1, groups_most + 1):

        @pl.when(groups == most)
        def _():
            drain(total, most * (width - 1), scatter_send)
            drain(total, most * (width - 1), return_send)
            drain(total, most * width, gather_recv)


def by_owner(plan, flip, ident, table, pieces, moments):
    blocks_all, rows, columns = pieces.shape
    width, items = plan.width, plan.items
    groups = plan.full // width
    low = jnp.bfloat16
    return pl.pallas_call(
        functools.partial(owner_kernel, plan, flip, rows),
        out_shape=jax.ShapeDtypeStruct((blocks_all, rows, columns), low),
        in_specs=[pl.BlockSpec(memory_space=pltpu.SMEM)] + [pl.BlockSpec(memory_space=pl.ANY)] * 2,
        out_specs=pl.BlockSpec(memory_space=pl.ANY),
        scratch_shapes=[
            pltpu.VMEM(pieces.shape, low),
            pltpu.VMEM(moments.shape, low),
            pltpu.VMEM((2, items, rows, columns), low),
            pltpu.VMEM((2, items, rows, columns), low),
            pltpu.VMEM((groups * width, rows, columns), low),
            pltpu.VMEM((groups, columns, columns), low),
            pltpu.VMEM((groups, columns, columns), low),
            pltpu.VMEM((columns, columns), jnp.float32),
            pltpu.VMEM((columns, columns), low),
            pltpu.VMEM((columns, columns), low),
            pltpu.SemaphoreType.DMA((2,)),
            pltpu.SemaphoreType.DMA((2,)),
            pltpu.SemaphoreType.DMA((2, items)),
            pltpu.SemaphoreType.DMA,
            pltpu.SemaphoreType.DMA((groups,)),
            pltpu.SemaphoreType.DMA,
            pltpu.SemaphoreType.DMA,
        ],
        compiler_params=pltpu.CompilerParams(
            collective_id=ident, has_side_effects=True, vmem_limit_bytes=50 * 1024 * 1024
        ),
        name=f"muon_owner_{ident}",
    )(table, pieces, moments)


def place_kernel(place, found, out_ref, held, wide, in_sem, out_sem):
    capacity = wide.shape[0]

    def bring(s):
        return pltpu.make_async_copy(found.at[place[0] + s], held.at[s], in_sem.at[s])

    def give(s):
        return pltpu.make_async_copy(wide.at[s], out_ref.at[0, s], out_sem.at[s])

    def start(s, carry):
        bring(s).start()
        return carry

    def widen(s, carry):
        bring(s).wait()
        piece = held[s].astype(jnp.float32)
        wide[s] = jnp.where(s < place[1], piece, jnp.zeros_like(piece))
        give(s).start()
        return carry

    def finish(s, carry):
        give(s).wait()
        return carry

    lax.fori_loop(0, capacity, start, 0, unroll=4)
    lax.fori_loop(0, capacity, widen, 0)
    lax.fori_loop(0, capacity, finish, 0, unroll=4)


def list_kernel(plans, capacity, owners, table, branch, place, order):
    n, last = len(plans) // 2, len(plans) // 2 - 1
    blocks_all = owners.shape[0]
    me = lax.axis_index("dp")

    def tally(b, held):
        return tuple(held[o] + (owners[b] == o).astype(jnp.int32) for o in range(n))

    held = lax.fori_loop(0, blocks_all, tally, (jnp.int32(0),) * n, unroll=8)
    fullest = jnp.int32(0)
    for o in range(n):
        fullest = jnp.where(held[o] == capacity, o, fullest)
    flip = fullest > last - fullest
    turn = jnp.minimum(fullest, last - fullest)
    ends = (held[0] >= plans[0].spare) & (held[last] >= plans[0].spare)
    base = []
    for o in range(n):
        total = jnp.int32(capacity)
        for other in range(n):
            if other != o:
                ahead = (flip == (other > o)) & (other != fullest)
                total = total + jnp.where(ahead, held[other], 0)
        base.append(jnp.where(fullest == o, 0, total))

    def put(b, free):
        owner = owners[b]
        where = free[n - 1]
        for o in range(n - 1):
            where = jnp.where(owner == o, free[o], where)
        order[where] = b
        return tuple(free[o] + (owner == o).astype(jnp.int32) for o in range(n))

    lax.fori_loop(0, blocks_all, put, tuple(base), unroll=8)
    begin, mine = base[n - 1], held[n - 1]
    for o in range(n - 1):
        begin, mine = jnp.where(me == o, base[o], begin), jnp.where(me == o, held[o], mine)
    at_last = jnp.where(flip, last - me, me) == last
    branch[0] = jnp.where(ends, fullest, fullest + n)
    place[0] = jnp.where(me != fullest, begin - capacity, 0)
    place[1] = mine

    nearer = (n + 1) // 2
    known = [[plan.positions() for plan in plans[k : k + nearer]] for k in (0, n)]
    for e in range(blocks_all):
        choice = [[], []]
        for side in range(2):
            for plan in range(2):
                lists = [known[plan][k][side] for k in range(nearer)]
                now = lists[0][min(e, len(lists[0]) - 1)]
                for k in range(1, nearer):
                    now = jnp.where(turn == k, lists[k][min(e, len(lists[k]) - 1)], now)
                choice[side].append(now)
        low, high = jnp.where(ends, choice[0][0], choice[0][1]), jnp.where(ends, choice[1][0], choice[1][1])
        table[e] = order[low]
        table[blocks_all + e] = order[high]
        here = jnp.where(at_last, high, low) - begin
        table[2 * blocks_all + e] = jnp.clip(here, 0, capacity - 1)
        table[3 * blocks_all + e] = ((here >= 0) & (here < mine)).astype(jnp.int32)


def routed(gradients, momentum, owners):
    n, width = lax.axis_size("dp"), lax.axis_size("tensor")
    pieces, moments = gradients[0], momentum[0]
    blocks_all, rows, columns = pieces.shape
    capacity = moments.shape[0]
    last = n - 1
    plans = [Plan(n, width, blocks_all, capacity, spare, min(p, last - p)) for spare in (width, 0) for p in range(n)]
    smem = pl.BlockSpec(memory_space=pltpu.SMEM)
    table, branch, place = pl.pallas_call(
        functools.partial(list_kernel, plans, capacity),
        out_shape=[jax.ShapeDtypeStruct((k,), jnp.int32) for k in (4 * blocks_all, 1, 2)],
        in_specs=[smem],
        out_specs=[smem] * 3,
        scratch_shapes=[pltpu.SMEM((blocks_all,), jnp.int32)],
        name="muon_lists",
    )(owners)
    branches = [functools.partial(by_owner, plan, k % n > last - k % n, k + 1) for k, plan in enumerate(plans)]
    found = lax.switch(branch[0], branches, table, pieces, moments)
    hbm = pl.BlockSpec(memory_space=pl.ANY)
    return pl.pallas_call(
        place_kernel,
        out_shape=jax.ShapeDtypeStruct((1, capacity, rows, columns), jnp.float32),
        in_specs=[smem, hbm],
        out_specs=hbm,
        scratch_shapes=[
            pltpu.VMEM((capacity, rows, columns), jnp.bfloat16),
            pltpu.VMEM((capacity, rows, columns), jnp.float32),
            pltpu.SemaphoreType.DMA((capacity,)),
            pltpu.SemaphoreType.DMA((capacity,)),
        ],
        compiler_params=pltpu.CompilerParams(vmem_limit_bytes=50 * 1024 * 1024),
        name="muon_place",
    )(place, found)


def choose(gradients, momentum, owners):
    n, width = lax.axis_size("dp"), lax.axis_size("tensor")
    blocks_all, rows = gradients.shape[1:3]
    capacity = momentum.shape[1]
    others = blocks_all - capacity
    even = blocks_all % (2 * width) == 0 and capacity % width == 0 and others % width == 0
    if n == 4 and even and width < others <= capacity and rows % 16 == 0 and others % (2 * width) == 0 and (blocks_all + 48) * capacity * blocks_all < 1 << 18 and width >= NS_TICKS:
        return routed(gradients, momentum, owners)
    return body(gradients, momentum, owners)


def solution(mesh):
    in_specs = (P("dp", None, "tensor", None), P("dp", None, "tensor", None), P())
    out_specs = P("dp", None, "tensor", None)
    return jax.shard_map(choose, mesh=mesh, in_specs=in_specs, out_specs=out_specs, check_vma=False)
```

```python
import functools
import math

import jax
import jax.numpy as jnp
from jax import lax
from jax.experimental import pallas as pl
from jax.experimental.pallas import tpu as pltpu
from jax.sharding import PartitionSpec as P

ITERS = 3


decay_rate = 0.95
newton_a = 3.4445
newton_b = -4.775
newton_c = 2.0315
norm_eps = 1e-07


def ranks_of(labels):
    length = labels.shape[0]
    places = jnp.arange(length, dtype=jnp.int32)
    earlier = (labels[None, :] == labels[:, None]) & (places[None, :] < places[:, None])
    return jnp.sum(earlier.astype(jnp.int32), axis=1)


def rows_at(array, index):
    count = array.shape[0]
    chosen = (index[:, None] == jnp.arange(count, dtype=jnp.int32)[None, :]).astype(array.dtype)
    picked = jnp.dot(chosen, array.reshape(count, -1), preferred_element_type=jnp.float32)
    return picked.astype(array.dtype).reshape((index.shape[0],) + array.shape[1:])


def dot(spec, left, right):
    return jnp.einsum(
        spec,
        left.astype(jnp.bfloat16),
        right.astype(jnp.bfloat16),
        preferred_element_type=jnp.float32,
    )


def iterate(blocks):
    widened = blocks.astype(jnp.float32) * (1.0 + decay_rate)
    lengths = jnp.sqrt(jnp.sum(widened * widened, axis=(1, 2), keepdims=True)) + norm_eps
    current = widened / lengths
    scale_up = math.sqrt(blocks.shape[1])
    for iteration in range(ITERS):
        squared = dot("kij,klj->kil", current, current)
        polynomial = newton_b * squared + newton_c * dot("kij,kjl->kil", squared, squared)
        current = newton_a * current + dot("kij,kjl->kil", polynomial, current)
    return current * scale_up


def body(gradients, momentum, owners):
    dp_count = lax.axis_size("dp")
    tp_count = lax.axis_size("tensor")
    my_group = lax.axis_index("dp")
    pieces = gradients[0]
    blocks_all, rows, columns = pieces.shape
    per_group = blocks_all // dp_count
    capacity = momentum.shape[1]
    slot_rank = ranks_of(owners)
    places = jnp.arange(blocks_all, dtype=jnp.int32)

    mine = owners == my_group
    moment = rows_at(momentum[0], jnp.minimum(slot_rank, capacity - 1))
    moment = jnp.where(mine[:, None, None], moment, jnp.zeros_like(moment)).astype(jnp.float32)
    ratio = decay_rate * decay_rate / (1.0 + decay_rate)
    folded = (pieces.astype(jnp.float32) + ratio * moment).astype(jnp.bfloat16)
    held = lax.psum_scatter(folded, "dp", scatter_dimension=0, tiled=True)

    per_device = (per_group + tp_count - 1) // tp_count
    padded_count = per_device * tp_count
    padded = jnp.pad(held, ((0, padded_count - per_group), (0, 0), (0, 0)))
    whole = lax.all_to_all(padded, "tensor", split_axis=0, concat_axis=1, tiled=True)
    finished = iterate(whole).astype(jnp.bfloat16)
    result = lax.all_to_all(finished, "tensor", split_axis=1, concat_axis=0, tiled=True)

    groups = jnp.arange(dp_count, dtype=jnp.int32)
    pair_most = (2 * per_group + dp_count - 1) // dp_count
    held_owner = lax.dynamic_slice_in_dim(owners, my_group * per_group, per_group)
    held_rank = ranks_of(held_owner)
    held_places = jnp.arange(per_group, dtype=jnp.int32)
    pair_ids = jnp.arange(pair_most, dtype=jnp.int32)
    matched = (held_owner[:, None, None] == groups[None, :, None]) & (
        held_rank[:, None, None] == pair_ids[None, None, :]
    )
    source = jnp.sum(jnp.where(matched, held_places[:, None, None], 0), axis=0).reshape(-1)
    outgoing = rows_at(result, source)
    outgoing = outgoing.reshape(dp_count, pair_most, rows, columns)
    incoming = lax.all_to_all(outgoing, "dp", split_axis=0, concat_axis=0, tiled=True)
    incoming = incoming.reshape(dp_count * pair_most, rows, columns)
    group_rank = ranks_of(owners * dp_count + places // per_group)
    position = places // per_group * pair_most + group_rank
    slot_ids = jnp.arange(capacity, dtype=jnp.int32)
    my_slots = mine[:, None] & (slot_rank[:, None] == slot_ids[None, :])
    occupied = jnp.any(my_slots, axis=0)
    arriving = jnp.sum(jnp.where(my_slots, position[:, None], 0), axis=0)
    chosen = rows_at(incoming, arriving).astype(jnp.float32)
    update = jnp.where(occupied[:, None, None], chosen, jnp.zeros_like(chosen))
    return update[None]


MESH = pl.DeviceIdType.MESH


AHEAD = 6
HOP = 4
SETTLE = 8
NS_TICKS = 2 * ITERS


def over(scaled, divisor):
    if isinstance(scaled, int):
        return scaled // divisor
    return (scaled * ((1 << 18) // divisor + 1)) >> 18


def at_most(limit, value):
    return min(limit, value) if isinstance(value, int) and isinstance(limit, int) else jnp.minimum(limit, value)


def pick(condition, yes, no):
    return (yes if condition else no) if isinstance(condition, bool) else jnp.where(condition, yes, no)


class Plan:
    def __init__(self, n, width, blocks_all, capacity, spare, place):
        self.n, self.width, self.place, self.last = n, width, place, n - 1
        self.full, self.spare = capacity, spare
        self.some = blocks_all - capacity - spare
        self.items = self.full + self.some
        self.batch = self.some // spare if spare else self.some
        self.early = HOP - 1 if place == 0 else 0

    def firsts(self, e):
        if self.place == 0:
            span = self.items - self.early
            return at_most(self.full, over(e * self.full + span - 1, span))
        return over(e * self.full, self.items)

    def split(self, e):
        p = self.firsts(e)
        return self.firsts(e + 1) > p, p, e - p

    def item(self, first_kind, u):
        full, some, items, early = self.full, self.some, self.items, self.early
        if self.place == 0:
            span, rest = items - early, some - early
            first = over(u * span, full)
            other = at_most(over((u + 1) * span + rest - 1, rest) - 1, full + u)
        else:
            first = over((u + 1) * items + full - 1, full) - 1
            other = over(u * items, some)
        return jnp.where(first_kind, first, other)

    def shuffled(self, r):
        group = over(r, self.batch + 1)
        k = r - group * (self.batch + 1)
        return pick(k == self.batch, self.some + group, group * self.batch + k)

    def positions(self):
        low, high = [], []
        for e in range(self.items):
            is_first, p, q = self.split(e)
            low.append(p if is_first else self.full + q)
            if self.place == 0:
                high.append(self.full + min(self.shuffled(p), self.some + self.spare - 1))
            else:
                high.append(p if is_first else self.full + (self.some + q if q < self.spare else q))
        return low, high

    def targets(self, d, is_first):
        if self.place == 0:
            return jnp.where(is_first, 0, 1) if d == 0 else self.last
        return jnp.where(is_first, self.place, 0 if d == 0 else self.last)

    def carried(self, d, is_first):
        return is_first if self.place == 0 and d == 1 else True

    def works_on_firsts(self, f):
        return (f == 0) | (f == self.last) if self.place == 0 else f == self.place

    def skipped(self, f):
        if self.place == 0:
            return 0
        return jnp.where((f == 0) | (f == self.last) | (f == self.place), 0, self.spare)

    def landing(self, f, u):
        if self.place == 0:
            return jnp.where(f == self.last, self.shuffled(u), u)
        q = u + self.skipped(f)
        return jnp.where((f == self.last) & (q < self.spare), q + self.some, q)

    def other_item(self, e, q):
        if self.place == 0:
            return self.item(True, q + over(q, self.batch))
        return e


def owner_kernel(
    plan, flip, rows, table, g_hbm, m_hbm, out_ref,
    g_ref, m_ref, arrived, partial, total, whole, ready, current, low_current, low_poly,
    load_sem, chain_send, chain_recv, scatter_send, scatter_recv, return_send, gather_recv,
):
    n, width, items = plan.n, plan.width, plan.items
    stride = g_ref.shape[0]
    columns = g_ref.shape[2]
    z, t = lax.axis_index("dp"), lax.axis_index("tensor")
    f = n - 1 - z if flip else z
    step = (1, -1) if flip else (-1, 1)
    groups_most = whole.shape[0]
    low = jnp.bfloat16

    load_g = pltpu.make_async_copy(g_hbm, g_ref, load_sem.at[0])
    load_m = pltpu.make_async_copy(m_hbm, m_ref, load_sem.at[1])
    load_g.start()
    load_m.start()

    barrier = pltpu.get_barrier_semaphore()

    @pl.when(z > 0)
    def _():
        pl.semaphore_signal(barrier, inc=1, device_id=(z - 1, t), device_id_type=MESH)

    @pl.when(z < n - 1)
    def _():
        pl.semaphore_signal(barrier, inc=1, device_id=(z + 1, t), device_id_type=MESH)

    def greet(k, carry):
        peer = lax.rem(t + k, width)
        pl.semaphore_signal(barrier, inc=1, device_id=(z, peer), device_id_type=MESH)
        return carry

    lax.fori_loop(1, width, greet, 0)
    pl.semaphore_wait(barrier, jnp.where((z == 0) | (z == n - 1), width, width + 1))
    load_g.wait()

    on_firsts = plan.works_on_firsts(f)
    skipped = plan.skipped(f)
    count = jnp.where(on_firsts, plan.full, plan.some - skipped)
    groups = count // width
    lag_low = HOP * (n - 1 - f)
    lag_high = HOP * f
    lag = jnp.where(f == 0, lag_low, jnp.where(f == n - 1, lag_high, jnp.maximum(lag_low, lag_high)))

    def my_rows(place):
        return pl.ds(pl.multiple_of(place * rows, rows), rows)

    spread = width // 2
    my_turn = t // 2 + lax.rem(t, 2) * spread

    def peer_of(u):
        k = lax.rem(u, width)
        return lax.rem(k, spread) * 2 + k // spread

    def chain_copy(d, e):
        return pltpu.make_async_remote_copy(
            src_ref=partial.at[d, e],
            dst_ref=arrived.at[d, e],
            send_sem=chain_send.at[d],
            recv_sem=chain_recv.at[d, e],
            device_id=(z + step[d], t),
            device_id_type=MESH,
        )

    def scatter_copy(u, peer):
        j = u // width
        return pltpu.make_async_remote_copy(
            src_ref=total.at[u],
            dst_ref=whole.at[j, my_rows(t)],
            send_sem=scatter_send,
            recv_sem=scatter_recv.at[j],
            device_id=(z, peer),
            device_id_type=MESH,
        )

    def return_copy(u, peer):
        j = u // width
        return pltpu.make_async_remote_copy(
            src_ref=ready.at[j, my_rows(peer)],
            dst_ref=out_ref.at[plan.landing(f, u)],
            send_sem=return_send,
            recv_sem=gather_recv,
            device_id=(z, peer),
            device_id_type=MESH,
        )

    def takes_part(d, e):
        is_first = plan.split(e)[0]
        target = plan.targets(d, is_first)
        inside = (e >= 0) & (e < items) & plan.carried(d, is_first)
        if d == 0:
            return inside & (f >= target) & (f < n - 1), inside & (f > target)
        return inside & (f <= target) & (f > 0), inside & (f < target)

    def flow(d, e):
        receives, sends = takes_part(d, e)
        blocks = d * stride + e

        @pl.when(receives)
        def _():
            chain_copy(d, e).wait_recv()

        @pl.when(sends & receives)
        def _():
            mixed = g_ref[table[blocks]].astype(jnp.float32) + arrived[d, e].astype(jnp.float32)
            partial[d, e] = mixed.astype(low)

        @pl.when(sends & jnp.logical_not(receives))
        def _():
            partial[d, e] = g_ref[table[blocks]]

        @pl.when(sends)
        def _():
            chain_copy(d, e).start()

    def candidate(e, u):
        def own(d):
            weight = table[3 * stride + e].astype(jnp.float32) * (decay_rate * decay_rate / (1.0 + decay_rate))
            moment = m_ref[table[2 * stride + e]].astype(jnp.float32)
            return g_ref[table[d * stride + e]].astype(jnp.float32) + weight * moment

        @pl.when(f == 0)
        def _():
            total[u] = (own(0) + arrived[0, e].astype(jnp.float32)).astype(low)

        @pl.when(f == n - 1)
        def _():
            total[u] = (own(1) + arrived[1, e].astype(jnp.float32)).astype(low)

        @pl.when((f > 0) & (f < n - 1))
        def _():
            twin = plan.other_item(e, u + skipped)
            both = arrived[0, e].astype(jnp.float32) + arrived[1, twin].astype(jnp.float32)
            total[u] = (own(0) + both).astype(low)

        peer = peer_of(u)

        @pl.when(peer == t)
        def _():
            whole[u // width, my_rows(t)] = total[u]

        @pl.when(peer != t)
        def _():
            scatter_copy(u, peer).start()

    def begin_block(j):
        most = pl.ds(0, (width - 1) * rows)
        pltpu.make_async_copy(ready.at[j, most], whole.at[j, most], scatter_recv.at[j]).wait()
        widened = whole[j].astype(jnp.float32) * (1.0 + decay_rate)
        length = jnp.sqrt(jnp.sum(widened * widened)) + norm_eps
        start = widened / length
        current[...] = start
        low_current[...] = start.astype(low)

    def make_polynomial():
        now = low_current[...]
        squared = lax.dot_general(now, now, (((1,), (1,)), ((), ())), preferred_element_type=jnp.float32)
        low_squared = squared.astype(low)
        polynomial = newton_b * squared + newton_c * jnp.dot(
            low_squared, low_squared, preferred_element_type=jnp.float32
        )
        low_poly[...] = polynomial.astype(low)

    def apply_polynomial():
        later = newton_a * current[...] + jnp.dot(
            low_poly[...], low_current[...], preferred_element_type=jnp.float32
        )
        current[...] = later
        low_current[...] = later.astype(low)

    def finish_block(j):
        ready[j] = (current[...] * math.sqrt(columns)).astype(low)
        u = j * width + my_turn

        def give(k, carry):
            return_copy(u, lax.rem(t + k, width)).start()
            return carry

        pltpu.make_async_copy(
            ready.at[j, my_rows(t)], out_ref.at[plan.landing(f, u)], gather_recv
        ).start()
        lax.fori_loop(1, width, give, 0)

    def tick(moment, carry):
        i = moment - AHEAD

        @pl.when(i == 0)
        def _():
            load_m.wait()

        flow(0, i - lag_low + jnp.where(f == n - 1, AHEAD, 0))
        flow(1, i - lag_high + jnp.where(f == 0, AHEAD, 0))
        e = i - lag
        is_first, p, q = plan.split(e)
        u = jnp.where(on_firsts, p, q - skipped)

        @pl.when((is_first == on_firsts) & (e >= 0) & (e < items) & (u >= 0))
        def _():
            candidate(e, u)

        since = jnp.maximum(e - SETTLE, -1)
        firsts = plan.firsts(since + 1)
        known = jnp.minimum(jnp.where(on_firsts, firsts, since + 1 - firsts - skipped), count)
        j = jnp.maximum(known - 1 - my_turn, 0) // width
        phase = since - plan.item(on_firsts, j * width + my_turn + jnp.where(on_firsts, 0, skipped))
        active = (known > my_turn) & (phase < NS_TICKS)

        @pl.when(active & (phase == 0))
        def _():
            begin_block(j)

        @pl.when(active & (phase % 2 == 0))
        def _():
            make_polynomial()

        @pl.when(active & (phase % 2 == 1))
        def _():
            apply_polynomial()

        @pl.when(active & (phase == NS_TICKS - 1))
        def _():
            finish_block(j)

        return carry

    lax.fori_loop(0, AHEAD + items + HOP * (n - 1) + SETTLE + NS_TICKS, tick, 0)

    def drain(held, amount, sem):
        part = held.at[pl.ds(0, amount)]
        pltpu.make_async_copy(part, part, sem).wait()

    for d in range(2):
        sends = []
        for is_first in (True, False):
            target = plan.targets(d, is_first)
            sends.append(plan.carried(d, is_first) & (f > target if d == 0 else f < target))

        for kinds, amount in (((True, True), plan.items), ((True, False), plan.full), ((False, True), plan.some)):

            @pl.when((sends[0] == kinds[0]) & (sends[1] == kinds[1]))
            def _():
                drain(partial.at[d], amount, chain_send.at[d])

    for most in range(1, groups_most + 1):

        @pl.when(groups == most)
        def _():
            drain(total, most * (width - 1), scatter_send)
            drain(total, most * (width - 1), return_send)
            drain(total, most * width, gather_recv)


def by_owner(plan, flip, ident, table, pieces, moments):
    blocks_all, rows, columns = pieces.shape
    width, items = plan.width, plan.items
    groups = plan.full // width
    low = jnp.bfloat16
    return pl.pallas_call(
        functools.partial(owner_kernel, plan, flip, rows),
        out_shape=jax.ShapeDtypeStruct((blocks_all, rows, columns), low),
        in_specs=[pl.BlockSpec(memory_space=pltpu.SMEM)] + [pl.BlockSpec(memory_space=pl.ANY)] * 2,
        out_specs=pl.BlockSpec(memory_space=pl.ANY),
        scratch_shapes=[
            pltpu.VMEM(pieces.shape, low),
            pltpu.VMEM(moments.shape, low),
            pltpu.VMEM((2, items, rows, columns), low),
            pltpu.VMEM((2, items, rows, columns), low),
            pltpu.VMEM((groups * width, rows, columns), low),
            pltpu.VMEM((groups, columns, columns), low),
            pltpu.VMEM((groups, columns, columns), low),
            pltpu.VMEM((columns, columns), jnp.float32),
            pltpu.VMEM((columns, columns), low),
            pltpu.VMEM((columns, columns), low),
            pltpu.SemaphoreType.DMA((2,)),
            pltpu.SemaphoreType.DMA((2,)),
            pltpu.SemaphoreType.DMA((2, items)),
            pltpu.SemaphoreType.DMA,
            pltpu.SemaphoreType.DMA((groups,)),
            pltpu.SemaphoreType.DMA,
            pltpu.SemaphoreType.DMA,
        ],
        compiler_params=pltpu.CompilerParams(
            collective_id=ident, has_side_effects=True, vmem_limit_bytes=50 * 1024 * 1024
        ),
        name=f"muon_owner_{ident}",
    )(table, pieces, moments)


def place_kernel(place, found, out_ref, held, wide, in_sem, out_sem):
    capacity = wide.shape[0]

    def bring(s):
        return pltpu.make_async_copy(found.at[place[0] + s], held.at[s], in_sem.at[s])

    def give(s):
        return pltpu.make_async_copy(wide.at[s], out_ref.at[0, s], out_sem.at[s])

    def start(s, carry):
        bring(s).start()
        return carry

    def widen(s, carry):
        bring(s).wait()
        piece = held[s].astype(jnp.float32)
        wide[s] = jnp.where(s < place[1], piece, jnp.zeros_like(piece))
        give(s).start()
        return carry

    def finish(s, carry):
        give(s).wait()
        return carry

    lax.fori_loop(0, capacity, start, 0, unroll=4)
    lax.fori_loop(0, capacity, widen, 0)
    lax.fori_loop(0, capacity, finish, 0, unroll=4)


def list_kernel(plans, capacity, owners, table, branch, place, order):
    n, last = len(plans) // 2, len(plans) // 2 - 1
    blocks_all = owners.shape[0]
    me = lax.axis_index("dp")

    def tally(b, held):
        return tuple(held[o] + (owners[b] == o).astype(jnp.int32) for o in range(n))

    held = lax.fori_loop(0, blocks_all, tally, (jnp.int32(0),) * n, unroll=8)
    fullest = jnp.int32(0)
    for o in range(n):
        fullest = jnp.where(held[o] == capacity, o, fullest)
    flip = fullest > last - fullest
    turn = jnp.minimum(fullest, last - fullest)
    ends = (held[0] >= plans[0].spare) & (held[last] >= plans[0].spare)
    base = []
    for o in range(n):
        total = jnp.int32(capacity)
        for other in range(n):
            if other != o:
                ahead = (flip == (other > o)) & (other != fullest)
                total = total + jnp.where(ahead, held[other], 0)
        base.append(jnp.where(fullest == o, 0, total))

    def put(b, free):
        owner = owners[b]
        where = free[n - 1]
        for o in range(n - 1):
            where = jnp.where(owner == o, free[o], where)
        order[where] = b
        return tuple(free[o] + (owner == o).astype(jnp.int32) for o in range(n))

    lax.fori_loop(0, blocks_all, put, tuple(base), unroll=8)
    begin, mine = base[n - 1], held[n - 1]
    for o in range(n - 1):
        begin, mine = jnp.where(me == o, base[o], begin), jnp.where(me == o, held[o], mine)
    at_last = jnp.where(flip, last - me, me) == last
    branch[0] = jnp.where(ends, fullest, fullest + n)
    place[0] = jnp.where(me != fullest, begin - capacity, 0)
    place[1] = mine

    nearer = (n + 1) // 2
    known = [[plan.positions() for plan in plans[k : k + nearer]] for k in (0, n)]
    for e in range(blocks_all):
        choice = [[], []]
        for side in range(2):
            for plan in range(2):
                lists = [known[plan][k][side] for k in range(nearer)]
                now = lists[0][min(e, len(lists[0]) - 1)]
                for k in range(1, nearer):
                    now = jnp.where(turn == k, lists[k][min(e, len(lists[k]) - 1)], now)
                choice[side].append(now)
        low, high = jnp.where(ends, choice[0][0], choice[0][1]), jnp.where(ends, choice[1][0], choice[1][1])
        table[e] = order[low]
        table[blocks_all + e] = order[high]
        here = jnp.where(at_last, high, low) - begin
        table[2 * blocks_all + e] = jnp.clip(here, 0, capacity - 1)
        table[3 * blocks_all + e] = ((here >= 0) & (here < mine)).astype(jnp.int32)


def routed(gradients, momentum, owners):
    n, width = lax.axis_size("dp"), lax.axis_size("tensor")
    pieces, moments = gradients[0], momentum[0]
    blocks_all, rows, columns = pieces.shape
    capacity = moments.shape[0]
    last = n - 1
    plans = [Plan(n, width, blocks_all, capacity, spare, min(p, last - p)) for spare in (width, 0) for p in range(n)]
    smem = pl.BlockSpec(memory_space=pltpu.SMEM)
    table, branch, place = pl.pallas_call(
        functools.partial(list_kernel, plans, capacity),
        out_shape=[jax.ShapeDtypeStruct((k,), jnp.int32) for k in (4 * blocks_all, 1, 2)],
        in_specs=[smem],
        out_specs=[smem] * 3,
        scratch_shapes=[pltpu.SMEM((blocks_all,), jnp.int32)],
        name="muon_lists",
    )(owners)
    branches = [functools.partial(by_owner, plan, k % n > last - k % n, k + 1) for k, plan in enumerate(plans)]
    found = lax.switch(branch[0], branches, table, pieces, moments)
    hbm = pl.BlockSpec(memory_space=pl.ANY)
    return pl.pallas_call(
        place_kernel,
        out_shape=jax.ShapeDtypeStruct((1, capacity, rows, columns), jnp.float32),
        in_specs=[smem, hbm],
        out_specs=hbm,
        scratch_shapes=[
            pltpu.VMEM((capacity, rows, columns), jnp.bfloat16),
            pltpu.VMEM((capacity, rows, columns), jnp.float32),
            pltpu.SemaphoreType.DMA((capacity,)),
            pltpu.SemaphoreType.DMA((capacity,)),
        ],
        compiler_params=pltpu.CompilerParams(vmem_limit_bytes=50 * 1024 * 1024),
        name="muon_place",
    )(place, found)


def choose(gradients, momentum, owners):
    n, width = lax.axis_size("dp"), lax.axis_size("tensor")
    blocks_all, rows = gradients.shape[1:3]
    capacity = momentum.shape[1]
    others = blocks_all - capacity
    even = blocks_all % (2 * width) == 0 and capacity % width == 0 and others % width == 0
    if n == 4 and even and width < others <= capacity and rows % 16 == 0 and others % (2 * width) == 0 and (blocks_all + 48) * capacity * blocks_all < 1 << 18 and width >= NS_TICKS:
        return routed(gradients, momentum, owners)
    return body(gradients, momentum, owners)


def solution(mesh):
    in_specs = (P("dp", None, "tensor", None), P("dp", None, "tensor", None), P())
    out_specs = P("dp", None, "tensor", None)
    return jax.shard_map(choose, mesh=mesh, in_specs=in_specs, out_specs=out_specs, check_vma=False)
```
